32 devices in a mesh: groups: 2 (over y), seq: 8 (over z, core), section: 2 (over x), tp: 1.
Axes of the slice: x: 2, y: 2, z: 4, core: 2. Of those that a mesh axis runs over, the one named last changes fastest.
Arguments:
- stream: bfloat16 [4, 512, 1536], P('groups', 'seq', 'tp'), parts along dimension 0, may hold values from -30 to 30
- set_views: int32 [4, 6], P('groups'), parts along dimension 0, may hold values from 1 to 2, 8 in all within a row
- modulation: bfloat16 [2, 4, 6, 2, 1536], P('section', 'groups', None, None, 'tp'), parts along dimension 1, may hold values from -2.5 to 2.5
- set_gate: bfloat16 [2, 4, 6, 1536], P('section', 'groups', None, 'tp'), parts along dimension 1, may hold values from 0.5 to 1.5
- qkv_weight: bfloat16 [2, 1536, 3, 1536], P('section', 'seq', None, 'tp'), may hold values from -0.15625 to 0.15625
- norm_gain: float32 [2, 2, 128], P('section'), may hold values from 0.1 to 1.9
- out_weight: bfloat16 [2, 1536, 1536], P('section', None, 'tp'), may hold values from -0.15625 to 0.15625
Outputs:
- hidden: bfloat16 [2, 4, 512, 1536], P('section', 'groups', 'seq', 'tp'), parts along dimension 1
The draws below stay inside these ranges and needn't reach their ends.
There are 2 independent parts, one for each index of `groups`. The reference program is written for one: setup_inputs(seed, part) draws one part's arguments, and reference() takes and returns one part's arrays. A program takes and returns all parts, laid end to end along the dimension named above; an argument that names none is the same for every part. Nothing has to cross between parts.
Inputs may be any that keep to these rules, and one draw needn't show every extreme that they name: Each row of set_views sums to 8; every row has a set of 2 views.
All inputs are finite; a program needn't handle non-finite values.
Results may differ from the reference program's by a relative error of at most 0.01.
Values may be sent and summed in bfloat16 or wider, within the bound.
No kernel may reach another device: no remote copies, remote signals or barrier semaphores. Data moves between devices by JAX's collectives and lax.ppermute only.
A program may use at most 64 MiB of HBM per device.

```python
import math
import jax
import jax.numpy as jnp
import numpy as np
from jax import lax

HEADS = 12
HEAD_DIM = 128
CH = 1536
VIEW_TOK = 64
MICRO = 2
MOST_VIEWS = 2
REACH = 1
SETS = 6
TOKENS = 512
SECTIONS = 2
N_SEQ = 8


def draw_stream(key, part):
    element_key, column_key, row_key = jax.random.split(key, 3)
    elements = jax.random.truncated_normal(element_key, -4.0, 4.0, (MICRO, TOKENS, CH), jnp.float32)
    columns = jnp.exp(jax.random.uniform(column_key, (CH,), jnp.float32, math.log(0.3), math.log(3.0)))
    row_scales = jnp.exp(jax.random.uniform(row_key, (MICRO, TOKENS, 1), jnp.float32, math.log(0.5), math.log(2.0)))
    return (elements * columns * row_scales).astype(jnp.bfloat16)


def level_of(key, extent, cuts, least, top_value):
    gain, own = 1.0, jax.random.fold_in(key, 6)
    for dim, shards_of in cuts:
        draws = jnp.exp(jax.random.uniform(jax.random.fold_in(own, dim), (shards_of,), jnp.float32, least / len(cuts), top_value / len(cuts)))
        gain = gain * jnp.repeat(draws, extent[dim] // shards_of).reshape([-1 if axis == dim else 1 for axis in range(len(extent))])
    return gain


def length_profile(count, total, reach, slope):
    portions = [(1 << 20) // math.isqrt(rank ** slope) + 1 for rank in range(2, count + 1)]
    spare, holding = total - reach - (count - 1), [1] * (count - 1)
    while spare > 0:
        candidates = [i for i in range(count - 1) if holding[i] < reach]
        whole, remaining = sum([portions[i] for i in candidates]), spare
        for i in candidates:
            extra = min(reach - holding[i], max(1, remaining * portions[i] // whole), spare)
            holding[i] = holding[i] + extra
            spare = spare - extra
    return np.array([reach] + holding)


def ragged(stream_key, amount, total, limit, skew):
    if amount == 2:
        one = jax.random.randint(stream_key, (), max(1, total - limit), min(limit, total - 1) + 1)
        return jnp.stack([one, total - one])
    sizes = jnp.asarray(length_profile(amount, total, limit, skew), jnp.int32)
    pairs = (amount - 1) // 2
    donor, taker = sizes[1:1 + 2 * pairs:2], sizes[2:2 + 2 * pairs:2]
    room = jnp.minimum(donor - 1, limit - taker)
    passed = jax.random.randint(jax.random.fold_in(stream_key, 1), (pairs,), 0, 1 << 20) % (room + 1)
    sizes = sizes.at[1:1 + 2 * pairs:2].set(donor - passed).at[2:2 + 2 * pairs:2].set(taker + passed)
    return sizes[jax.random.permutation(jax.random.fold_in(stream_key, 2), amount)]


def bell_draw(key, extent, scale, reach, shards=(), kind=jnp.bfloat16):
    entries = jax.random.normal(key, extent, jnp.float32) * scale
    if len(shards) > 0:
        entries = level_of(key, extent, shards, -0.22, 0.18) * entries
    return jnp.clip(entries, min=-reach, max=reach).astype(kind)


def setup_inputs(seed: int = 0, part: int = 0) -> dict:
    key_list = jax.random.split(jax.random.key(seed), 8)
    part_keys = jax.random.split(jax.random.fold_in(key_list[7], part), 8)
    return {
        "stream": draw_stream(jax.random.fold_in(jax.random.fold_in(key_list[7], part), 71), part),
        "set_views": jax.vmap(lambda own: ragged(own, SETS, N_SEQ, MOST_VIEWS, 2))(jax.random.split(part_keys[1], MICRO)).reshape((MICRO, SETS)).astype(jnp.int32),
        "modulation": bell_draw(part_keys[2], (SECTIONS, MICRO, SETS, 2, CH), 0.5, 2.5, ((0, 2),)),
        "set_gate": jnp.clip(0.5 + 1.0 * jax.random.uniform(part_keys[3], (SECTIONS, MICRO, SETS, CH), jnp.float32) ** level_of(part_keys[3], (SECTIONS, MICRO, SETS, CH), ((0, 2),), -0.2, 0.2), 0.5, 1.5).astype(jnp.bfloat16),
        "qkv_weight": bell_draw(key_list[4], (SECTIONS, CH, 3, CH), CH ** -0.5, 0.15625, ((0, 2), (1, 8))),
        "norm_gain": jnp.clip(1.0 + 0.18 * jax.random.normal(key_list[5], (SECTIONS, 2, HEAD_DIM), jnp.float32), 0.1, 1.9),
        "out_weight": bell_draw(key_list[6], (SECTIONS, CH, CH), CH ** -0.5, 0.15625, ((0, 2),)),
    }


epsilon = 1e-06

def rounded(values):
    return lax.optimization_barrier(values.astype(jnp.bfloat16))

def view_sets(set_views):
    counts = set_views.astype(jnp.int32)
    starts = (jnp.cumsum(counts) - counts).astype(jnp.int32)
    position = jnp.arange(N_SEQ, dtype=jnp.int32)
    inside = (starts[None, :] <= position[:, None]).astype(jnp.int32)
    return (lax.optimization_barrier(jnp.sum(inside, axis=1)) - 1).astype(jnp.int32)

def unit_rms(values, scaling):
    return values * lax.rsqrt(lax.optimization_barrier(jnp.mean(values * values, axis=-1, keepdims=True)) + epsilon) * scaling

def one_block(current, set_views, modulation, set_gate, qkv_weight, norm_gain, out_weight):
    owners = view_sets(set_views)
    token_sets = jnp.repeat(owners, VIEW_TOK)
    widened = current.astype(jnp.float32)
    average = lax.optimization_barrier(jnp.mean(widened, axis=-1, keepdims=True))
    squares = lax.optimization_barrier(jnp.mean(widened * widened, axis=-1, keepdims=True))
    spread = squares - average * average
    per_token = modulation[token_sets].astype(jnp.float32)
    normed = rounded((widened - average) * lax.rsqrt(spread + epsilon) * (1.0 + per_token[:, 1]) + per_token[:, 0])
    projected = jnp.dot(normed, qkv_weight.reshape(CH, 3 * CH), preferred_element_type=jnp.float32).reshape(TOKENS, 3, HEADS, HEAD_DIM)
    gain_pair = norm_gain.astype(jnp.float32)
    queries = rounded(unit_rms(projected[:, 0], gain_pair[0]))
    keys_all = rounded(unit_rms(projected[:, 1], gain_pair[1]))
    values_all = rounded(projected[:, 2])
    margin = REACH * VIEW_TOK
    keys_pad = jnp.pad(keys_all, ((margin, margin), (0, 0), (0, 0)))
    values_pad = jnp.pad(values_all, ((margin, margin), (0, 0), (0, 0)))
    owners_pad = jnp.pad(owners, (REACH, REACH), constant_values=-1)
    window_keys = (2 * REACH + 1) * VIEW_TOK

    def per_view(view_index):
        first_row = (view_index * VIEW_TOK).astype(jnp.int32)
        query_block = lax.dynamic_slice_in_dim(queries, first_row, VIEW_TOK, 0).astype(jnp.float32)
        key_block = lax.dynamic_slice_in_dim(keys_pad, first_row, window_keys, 0).astype(jnp.float32)
        value_block = lax.dynamic_slice_in_dim(values_pad, first_row, window_keys, 0).astype(jnp.float32)
        nearby = lax.dynamic_slice_in_dim(owners_pad, view_index, 2 * REACH + 1, 0)
        own_set = lax.dynamic_index_in_dim(owners, view_index, 0, keepdims=False)
        visible = jnp.repeat((nearby == own_set).astype(jnp.float32), VIEW_TOK)
        scores = jnp.einsum('qhd,khd->hqk', query_block, key_block) * HEAD_DIM ** (-0.5)
        exponent = jnp.exp(scores) * visible
        denominator = lax.optimization_barrier(jnp.sum(exponent, axis=-1))
        weights = rounded(exponent).astype(jnp.float32)
        numerator = jnp.einsum('hqk,khd->qhd', weights, value_block)
        return (numerator / jnp.transpose(denominator)[:, :, None]).astype(jnp.bfloat16)
    attended = lax.map(per_view, jnp.arange(N_SEQ, dtype=jnp.int32)).reshape(TOKENS, HEADS * HEAD_DIM)
    mixed_out = jnp.dot(attended, out_weight, preferred_element_type=jnp.float32)
    gating = set_gate[token_sets].astype(jnp.float32)
    return (widened + gating * mixed_out).astype(jnp.bfloat16)

def reference(stream, set_views, modulation, set_gate, qkv_weight, norm_gain, out_weight):
    current = [stream[micro_index] for micro_index in range(MICRO)]
    layers = []
    for section_index in range(SECTIONS):
        current = [one_block(current[micro_index], set_views[micro_index], modulation[section_index, micro_index], set_gate[section_index, micro_index], qkv_weight[section_index], norm_gain[section_index], out_weight[section_index]) for micro_index in range(MICRO)]
        layers.append(jnp.stack(current))
    return jnp.stack(layers)
```

```python
import functools

import jax
import jax.numpy as jnp
from jax import lax
from jax.experimental import pallas as pl
from jax.experimental.pallas import tpu as pltpu
from jax.sharding import PartitionSpec as P

REACH = 1


epsilon = 1e-06


def view_sets(set_views, count):
    amount = set_views.shape[0]
    before = jnp.arange(amount)[:, None] > jnp.arange(amount)[None, :]
    starts = jnp.sum(jnp.where(before, set_views[None, :], 0), axis=1)
    position = jnp.arange(count, dtype=jnp.int32)
    inside = (starts[None, :] <= position[:, None]).astype(jnp.int32)
    return jnp.sum(inside, axis=1) - 1


def attend_kernel(
    table,
    own,
    pair,
    halo,
    pair_halo,
    modulation,
    gains,
    home,
    home_pair,
    o_first,
    o_mid1,
    o_end1,
    o_mid2,
    o_end2,
    d_first,
    d_mid1,
    d_end1,
    d_mid2,
    d_end2,
    att_own,
    att_pair,
    weights,
    normed,
    sems,
):
    micro_count, view_tok, width = own.shape
    rows = weights.shape[0] // 8
    part = weights.shape[1] // 3
    head = gains.shape[1]
    middle = table[0]

    def piece(source, index):
        start = pl.multiple_of(table[1 + index] * rows, rows)
        return pltpu.make_async_copy(
            source, weights.at[pl.ds(start, rows), :], sems.at[index]
        )

    def load(index, mid, end):
        @pl.when(middle == 1)
        def _():
            piece(mid, index).start()

        @pl.when(middle == 0)
        def _():
            piece(end, index).start()

    piece(home, 0).start()
    piece(home_pair, 1).start()
    piece(o_first, 2).start()
    piece(d_first, 3).start()
    load(4, o_mid1, o_end1)
    load(5, d_mid1, d_end1)
    load(6, o_mid2, o_end2)
    load(7, d_mid2, d_end2)

    half = 2 * micro_count * view_tok
    for slot, source in enumerate((own, pair, halo, pair_halo)):
        for m in range(micro_count):
            wide = source[m].astype(jnp.float32)
            average = jnp.mean(wide, axis=-1, keepdims=True)
            squares = jnp.mean(wide * wide, axis=-1, keepdims=True)
            spread = squares - average * average
            factors = modulation[m, table[9 + 4 * m + slot]].astype(jnp.float32)
            value = (wide - average) * lax.rsqrt(spread + epsilon) * (
                1.0 + factors[1:2]
            ) + factors[0:1]
            first = half * (slot // 2) + (2 * m + slot % 2) * view_tok
            normed[first : first + view_tok, :] = value.astype(jnp.bfloat16)

    for index in range(8):
        piece(home, index).wait()

    two = 2 * view_tok
    low_row = lax.broadcasted_iota(jnp.int32, (two, two), 0) < view_tok
    low_col = lax.broadcasted_iota(jnp.int32, (two, two), 1) < view_tok
    near_masks, far_masks = [], []
    for m in range(micro_count):
        base = 9 + 4 * micro_count + 3 * m
        together = jnp.where(table[base] == 1, 1.0, 0.0)
        below = jnp.where(table[base + 1] == 1, 1.0, 0.0)
        above = jnp.where(table[base + 2] == 1, 1.0, 0.0)
        near_masks.append(jnp.where(low_row == low_col, 1.0, together))
        far_masks.append(
            jnp.where(
                low_row & low_col,
                below,
                jnp.where(low_row | low_col, 0.0, above),
            )
        )

    def unit(values, gain):
        return (
            values
            * lax.rsqrt(jnp.mean(values * values, axis=-1, keepdims=True) + epsilon)
            * gain
        ).astype(jnp.bfloat16)

    def dot(a, b):
        return jnp.dot(a, b, preferred_element_type=jnp.float32)

    def dot_t(a, b):
        return lax.dot_general(
            a, b, (((1,), (1,)), ((), ())), preferred_element_type=jnp.float32
        )

    query_gain = gains[0:1, :]
    key_gain = gains[1:2, :]
    block = 2 * head

    def heads(step, carry):
        offset = pl.multiple_of(step * block, block)
        raw_q = dot(normed[0:half, :], weights[:, pl.ds(offset, block)])
        raw_k = dot(normed[...], weights[:, pl.ds(part + offset, block)])
        raw_v = dot(normed[...], weights[:, pl.ds(2 * part + offset, block)])
        outs = [[None] * 2 for _ in range(micro_count)]
        for i in range(2):
            cols = slice(i * head, (i + 1) * head)
            queries = unit(raw_q[:, cols], query_gain)
            keys = unit(raw_k[:, cols], key_gain)
            values = raw_v[:, cols].astype(jnp.bfloat16)
            for m in range(micro_count):
                near = slice(m * two, (m + 1) * two)
                far = slice(half + m * two, half + (m + 1) * two)
                q = queries[near]
                scale = head ** (-0.5)
                e_near = jnp.exp(dot_t(q, keys[near]) * scale) * near_masks[m]
                e_far = jnp.exp(dot_t(q, keys[far]) * scale) * far_masks[m]
                total = jnp.sum(e_near, axis=-1, keepdims=True) + jnp.sum(
                    e_far, axis=-1, keepdims=True
                )
                mixed = dot(e_near.astype(jnp.bfloat16), values[near]) + dot(
                    e_far.astype(jnp.bfloat16), values[far]
                )
                outs[m][i] = (mixed / total).astype(jnp.bfloat16)
        for m in range(micro_count):
            joined = jnp.concatenate(outs[m], axis=1)
            att_own[m, :, pl.ds(offset, block)] = joined[:view_tok]
            att_pair[m, :, pl.ds(offset, block)] = joined[view_tok:]
        return carry

    lax.fori_loop(0, part // block, heads, 0)


def project_kernel(
    table, att_own, att_got, stream, gates, out_weight, result, weights, sems
):
    micro_count, view_tok, part = att_own.shape
    width = out_weight.shape[1]
    mine = table[0]
    blocks = sems.shape[0]
    block = width // blocks

    def piece(index):
        return pltpu.make_async_copy(
            out_weight.at[:, pl.ds(index * block, block)],
            weights.at[:, pl.ds(index * block, block)],
            sems.at[index],
        )

    for index in range(blocks):
        piece(index).start()
    tokens = micro_count * view_tok
    here = att_own[...].reshape(tokens, part)
    there = att_got[...].reshape(tokens, part)
    first = pl.multiple_of(mine * part, part)
    second = pl.multiple_of((1 - mine) * part, part)
    for index in range(blocks):
        piece(index).wait()
        cols = slice(index * block, (index + 1) * block)
        mixed = jnp.dot(
            here, weights[pl.ds(first, part), cols], preferred_element_type=jnp.float32
        ) + jnp.dot(
            there,
            weights[pl.ds(second, part), cols],
            preferred_element_type=jnp.float32,
        )
        for m in range(micro_count):
            gate = gates[m, table[1 + m]][:, cols].astype(jnp.float32)
            result[m, :, cols] = (
                stream[m, :, cols].astype(jnp.float32)
                + gate * mixed[m * view_tok : (m + 1) * view_tok]
            ).astype(jnp.bfloat16)


def paired_body(
    stream, set_views, modulation, set_gate, qkv_weight, norm_gain, out_weight
):
    micro_count, view_tok, width = stream.shape
    head = norm_gain.shape[2]
    part = width // 2
    rows = qkv_weight.shape[1]
    seq_count = lax.axis_size("seq")
    section_count = lax.axis_size("section")
    group = lax.axis_index("groups")
    place = lax.axis_index("seq")
    core = place % 2
    chip = place // 2
    mine = core ^ group
    line_axes = ("groups", "seq")

    def along(steps):
        return [
            (g * seq_count + 2 * a + c, g * seq_count + 2 * b + c)
            for g in range(2)
            for c in range(2)
            for a, b in steps
        ]

    def across(chips):
        return [
            (g * seq_count + 2 * a + c, (1 - g) * seq_count + 2 * a + 1 - c)
            for g in range(2)
            for c in range(2)
            for a in chips
        ]

    def send(value, pairs):
        return lax.ppermute(value, line_axes, pairs)

    swap_cores = [(i, i ^ 1) for i in range(seq_count)]
    swap_edges = [(i, i + 1) for i in range(1, seq_count - 1, 2)] + [
        (i + 1, i) for i in range(1, seq_count - 1, 2)
    ]

    halves = qkv_weight[0].reshape(rows, 3, 2, part)
    home = lax.dynamic_index_in_dim(halves, mine, 2, False).reshape(rows, 3 * part)
    lent = lax.dynamic_index_in_dim(halves, 1 - mine, 2, False).reshape(rows, 3 * part)

    o_first = send(home, along([(0, 1), (1, 0), (2, 3), (3, 2)]))
    o_mid1 = send(home, along([(1, 2), (2, 1)]))
    home_pair = lax.ppermute(lent, "seq", swap_cores)
    o_mid2 = send(o_first, along([(1, 2), (2, 1)]))
    o_end1 = send(o_mid1, along([(1, 0), (2, 3)]))
    d_first = send(o_first, across(range(4)))
    d_mid1 = send(o_mid1, across([1, 2]))
    d_end1 = send(o_end1, across([0, 3]))
    o_end2 = send(o_mid2, along([(1, 0), (2, 3)]))
    d_mid2 = send(o_mid2, across([1, 2]))
    d_end2 = send(o_end2, across([0, 3]))

    middle = ((chip == 1) | (chip == 2)).astype(jnp.int32)
    first_chip = chip ^ 1
    second_chip = jnp.where(middle == 1, 3 - chip, chip ^ 2)
    third_chip = jnp.where(middle == 1, (3 - chip) ^ 1, 3 - chip)
    order = []
    for other in (chip, first_chip, second_chip, third_chip):
        order += [2 * other + core, 2 * other + 1 - core]

    owners = jnp.stack([view_sets(set_views[m], seq_count) for m in range(micro_count)])
    outward = jnp.where(core == 0, -1, 1)
    pair_place = place + outward * -1
    halo_place = place + outward
    pair_halo_place = pair_place - outward
    sets, masks = [], []

    def owner(m, where):
        return owners[m, jnp.clip(where, 0, seq_count - 1)]

    def inside(where):
        return (where >= 0) & (where < seq_count)

    for m in range(micro_count):
        own_set, pair_set = owner(m, place), owner(m, pair_place)
        halo_set, pair_halo_set = owner(m, halo_place), owner(m, pair_halo_place)
        sets += [own_set, pair_set, halo_set, pair_halo_set]
        masks += [
            own_set == pair_set,
            inside(halo_place) & (own_set == halo_set),
            inside(pair_halo_place) & (pair_set == pair_halo_set),
        ]
    table = jnp.stack(
        [middle] + order + sets + [m.astype(jnp.int32) for m in masks]
    ).astype(jnp.int32)
    gate_table = jnp.stack(
        [mine] + [owner(m, place) for m in range(micro_count)]
    ).astype(jnp.int32)
    gates = set_gate[0][:, :, None, :]

    vmem = pl.BlockSpec(memory_space=pltpu.VMEM)
    smem = pl.BlockSpec(memory_space=pltpu.SMEM)
    anywhere = pl.BlockSpec(memory_space=pl.ANY)
    half_shape = jax.ShapeDtypeStruct((micro_count, view_tok, part), jnp.bfloat16)
    attend = pl.pallas_call(
        attend_kernel,
        out_shape=(half_shape, half_shape),
        in_specs=[smem] + [vmem] * 6 + [anywhere] * 12,
        out_specs=(vmem, vmem),
        scratch_shapes=[
            pltpu.VMEM((width, 3 * part), jnp.bfloat16),
            pltpu.VMEM((4 * micro_count * view_tok, width), jnp.bfloat16),
            pltpu.SemaphoreType.DMA((8,)),
        ],
        compiler_params=pltpu.CompilerParams(vmem_limit_bytes=40 * 1024 * 1024),
        name="attend",
    )
    project = pl.pallas_call(
        project_kernel,
        out_shape=jax.ShapeDtypeStruct(stream.shape, jnp.bfloat16),
        in_specs=[smem] + [vmem] * 4 + [anywhere],
        out_specs=vmem,
        scratch_shapes=[
            pltpu.VMEM((width, width), jnp.bfloat16),
            pltpu.SemaphoreType.DMA((3,)),
        ],
        compiler_params=pltpu.CompilerParams(vmem_limit_bytes=24 * 1024 * 1024),
        name="project",
    )

    section_place = lax.axis_index("section")
    own = stream
    hidden = None
    for moment in range(section_count):
        halo = lax.ppermute(own, "seq", swap_edges)
        pair = lax.ppermute(own, "seq", swap_cores)
        pair_halo = lax.ppermute(halo, "seq", swap_cores)
        att_own, att_pair = attend(
            table,
            own,
            pair,
            halo,
            pair_halo,
            modulation[0],
            norm_gain[0],
            home,
            home_pair,
            o_first,
            o_mid1,
            o_end1,
            o_mid2,
            o_end2,
            d_first,
            d_mid1,
            d_end1,
            d_mid2,
            d_end2,
        )
        att_got = lax.ppermute(att_pair, "seq", swap_cores)
        result = project(gate_table, att_own, att_got, own, gates, out_weight[0])
        if moment == 0:
            hidden = result
        else:
            hidden = jnp.where(section_place == moment, result, hidden)
        if moment + 1 < section_count:
            own = lax.ppermute(
                result, "section", [(i, i + 1) for i in range(section_count - 1)]
            )
    return hidden[None]


def shifted(array, axis, by):
    size = lax.axis_size(axis)
    pairs = [(i, i + by) for i in range(size) if 0 <= i + by < size]
    return lax.ppermute(array, axis, pairs)


def unit_rms(values, scaling):
    return (
        values
        * lax.rsqrt(jnp.mean(values * values, axis=-1, keepdims=True) + epsilon)
        * scaling
    )


def general_body(
    stream, set_views, modulation, set_gate, qkv_weight, norm_gain, out_weight
):
    micro_count, view_tok, local_width = stream.shape
    head_size = norm_gain.shape[2]
    head_count = local_width // head_size
    seq_count = lax.axis_size("seq")
    section_count = lax.axis_size("section")
    seq_place = lax.axis_index("seq")
    section_place = lax.axis_index("section")
    full_width = local_width * lax.axis_size("tp")
    whole_qkv = lax.all_gather(qkv_weight[0], "seq", axis=0, tiled=True)
    qkv_flat = whole_qkv.reshape(whole_qkv.shape[0], 3 * local_width)
    gain_pair = norm_gain[0]
    out_rows = out_weight[0]
    score_scale = head_size ** (-0.5)
    offsets = list(range(-REACH, REACH + 1))
    ticks = micro_count + section_count - 1
    carried = jnp.zeros((view_tok, local_width), jnp.bfloat16)
    hidden = jnp.zeros((micro_count, view_tok, local_width), jnp.bfloat16)
    for moment in range(ticks):
        fresh_input = stream[min(moment, micro_count - 1)]
        section_input = jnp.where(section_place == 0, fresh_input, carried)
        micro_raw = moment - section_place
        micro_index = jnp.clip(micro_raw, 0, micro_count - 1)
        owners = view_sets(set_views[micro_index], seq_count)
        own_set = owners[seq_place]
        widened = section_input.astype(jnp.float32)
        totals, squares = lax.psum(
            (jnp.sum(widened, axis=1), jnp.sum(widened * widened, axis=1)), "tp"
        )
        average = (totals / full_width)[:, None]
        spread = (squares / full_width)[:, None] - average * average
        factors = modulation[0, micro_index, own_set].astype(jnp.float32)
        normed = (
            (widened - average) * lax.rsqrt(spread + epsilon) * (1.0 + factors[1])
            + factors[0]
        ).astype(jnp.bfloat16)
        projected = jnp.dot(
            lax.all_gather(normed, "tp", axis=1, tiled=True),
            qkv_flat,
            preferred_element_type=jnp.float32,
        )
        parts = projected.reshape(view_tok, 3, head_count, head_size)
        queries = unit_rms(parts[:, 0], gain_pair[0]).astype(jnp.bfloat16)
        keys_here = unit_rms(parts[:, 1], gain_pair[1]).astype(jnp.bfloat16)
        values_here = parts[:, 2].astype(jnp.bfloat16)
        payload = jnp.stack(
            [
                keys_here.reshape(view_tok, local_width),
                values_here.reshape(view_tok, local_width),
            ]
        )
        arrived = [shifted(payload, "seq", 1), payload, shifted(payload, "seq", -1)]
        key_list = [r[0].reshape(view_tok, head_count, head_size) for r in arrived]
        value_list = [r[1].reshape(view_tok, head_count, head_size) for r in arrived]
        visible = []
        for offset in offsets:
            neighbour = seq_place + offset
            in_range = (neighbour >= 0) & (neighbour < seq_count)
            same_set = owners[jnp.clip(neighbour, 0, seq_count - 1)] == own_set
            visible.append((in_range & same_set).astype(jnp.float32))
        keys_cat = jnp.concatenate(key_list, axis=0)
        values_cat = jnp.concatenate(value_list, axis=0)
        mask_row = jnp.repeat(jnp.stack(visible), view_tok)
        scores = (
            jnp.einsum(
                "qhd,khd->hqk", queries, keys_cat, preferred_element_type=jnp.float32
            )
            * score_scale
        )
        exponent = jnp.exp(scores) * mask_row
        denominator = jnp.sum(exponent, axis=-1)
        numerator = jnp.einsum(
            "hqk,khd->qhd",
            exponent.astype(jnp.bfloat16),
            values_cat,
            preferred_element_type=jnp.float32,
        )
        attended = (
            (numerator / jnp.transpose(denominator)[:, :, None])
            .astype(jnp.bfloat16)
            .reshape(view_tok, local_width)
        )
        mixed_out = jnp.dot(
            lax.all_gather(attended, "tp", axis=1, tiled=True),
            out_rows,
            preferred_element_type=jnp.float32,
        )
        gating = set_gate[0, micro_index, own_set].astype(jnp.float32)
        result = (widened + gating * mixed_out).astype(jnp.bfloat16)
        in_range = (micro_raw >= 0) & (micro_raw < micro_count)
        hidden = jnp.where(in_range, hidden.at[micro_index].set(result), hidden)
        if moment + 1 < ticks:
            carried = shifted(result, "section", 1)
    return hidden[None]


def solution(mesh):
    placed = (
        P("groups", "seq", "tp"),
        P("groups", None),
        P("section", "groups", None, None, "tp"),
        P("section", "groups", None, "tp"),
        P("section", "seq", None, "tp"),
        P("section", None, None),
        P("section", None, "tp"),
    )
    sizes = mesh.shape
    paired = sizes["tp"] == 1 and sizes["groups"] == 2 and sizes["seq"] == 8
    return jax.shard_map(
        paired_body if paired else general_body,
        mesh=mesh,
        in_specs=placed,
        out_specs=P("section", "groups", "seq", "tp"),
        check_vma=False,
    )
```

```python
import functools

import jax
import jax.numpy as jnp
from jax import lax
from jax.experimental import pallas as pl
from jax.experimental.pallas import tpu as pltpu
from jax.sharding import PartitionSpec as P

REACH = 1


epsilon = 1e-06


def view_sets(set_views, count):
    amount = set_views.shape[0]
    before = jnp.arange(amount)[:, None] > jnp.arange(amount)[None, :]
    starts = jnp.sum(jnp.where(before, set_views[None, :], 0), axis=1)
    position = jnp.arange(count, dtype=jnp.int32)
    inside = (starts[None, :] <= position[:, None]).astype(jnp.int32)
    return jnp.sum(inside, axis=1) - 1


def owner_of(views, m, place):
    start, owner = jnp.int32(0), jnp.int32(-1)
    for j in range(views.shape[1]):
        owner = owner + jnp.where(start <= place, 1, 0)
        start = start + views[m, j]
    return owner


def attend_table(views):
    count = lax.axis_size("seq")
    place = lax.axis_index("seq")
    core = place % 2
    chip = place // 2
    middle = (chip == 1) | (chip == 2)
    others = (
        chip,
        chip + 1 - 2 * (chip % 2),
        jnp.where(middle, 3 - chip, (chip + 2) % 4),
        jnp.where(middle, jnp.where(chip == 1, 3, 0), 3 - chip),
    )
    order = []
    for other in others:
        order += [2 * other + core, 2 * other + 1 - core]
    outward = 2 * core - 1
    pair_place = place - outward
    halo_place = place + outward
    pair_halo_place = pair_place - outward
    places = (place, pair_place, halo_place, pair_halo_place)
    sets, masks = [], []
    for m in range(views.shape[0]):
        found = [
            owner_of(views, m, jnp.clip(where, 0, count - 1)) for where in places
        ]
        sets.append(found)
        masks.append(
            (
                found[0] == found[1],
                (halo_place >= 0) & (halo_place < count) & (found[0] == found[2]),
                (pair_halo_place >= 0)
                & (pair_halo_place < count)
                & (found[1] == found[3]),
            )
        )
    return order, sets, masks


def attend_kernel(*refs):
    views, own, pair, halo, pair_halo, modulation_src, gains = refs[:7]
    pieces = refs[7:31]
    att_own, att_pair = refs[31:33]
    weights, normed, streams, modulation, sems, stream_sems = refs[33:]
    _, micro_count, view_tok, width = streams.shape
    rows = weights.shape[0] // 8
    part = weights.shape[1] // 3
    head = gains.shape[1]
    order, sets, masks = attend_table(views)

    def piece(index):
        start = pl.multiple_of(order[index // 3] * rows, rows)
        return pltpu.make_async_copy(
            pieces[index],
            weights.at[pl.ds(start, rows), pl.ds(index % 3 * part, part)],
            sems.at[index],
        )

    sources = (own, pair, halo, pair_halo)
    scales = pltpu.make_async_copy(modulation_src, modulation, stream_sems.at[4])
    incoming = [
        pltpu.make_async_copy(sources[slot], streams.at[slot], stream_sems.at[slot])
        for slot in range(4)
    ]
    scales.start()
    for slot in range(4):
        incoming[slot].start()
    for index in range(24):
        piece(index).start()

    half = 2 * micro_count * view_tok
    scales.wait()
    for slot in range(4):
        incoming[slot].wait()
        for m in range(micro_count):
            wide = streams[slot, m].astype(jnp.float32)
            average = jnp.mean(wide, axis=-1, keepdims=True)
            squares = jnp.mean(wide * wide, axis=-1, keepdims=True)
            spread = squares - average * average
            factors = modulation[m, sets[m][slot]].astype(jnp.float32)
            value = (wide - average) * lax.rsqrt(spread + epsilon) * (
                1.0 + factors[1:2]
            ) + factors[0:1]
            first = half * (slot // 2) + (2 * m + slot % 2) * view_tok
            normed[first : first + view_tok, :] = value.astype(jnp.bfloat16)

    for index in range(24):
        piece(index).wait()

    two = 2 * view_tok
    low_row = lax.broadcasted_iota(jnp.int32, (two, two), 0) < view_tok
    low_col = lax.broadcasted_iota(jnp.int32, (two, two), 1) < view_tok
    near_masks, far_masks = [], []
    for m in range(micro_count):
        together, below, above = (jnp.where(mask, 1.0, 0.0) for mask in masks[m])
        near_masks.append(jnp.where(low_row == low_col, 1.0, together))
        far_masks.append(
            jnp.where(
                low_row & low_col,
                below,
                jnp.where(low_row | low_col, 0.0, above),
            )
        )

    def unit(values, gain):
        return (
            values
            * lax.rsqrt(jnp.mean(values * values, axis=-1, keepdims=True) + epsilon)
            * gain
        ).astype(jnp.bfloat16)

    def dot(a, b):
        return jnp.dot(a, b, preferred_element_type=jnp.float32)

    def dot_t(a, b):
        return lax.dot_general(
            a, b, (((1,), (1,)), ((), ())), preferred_element_type=jnp.float32
        )

    query_gain = gains[0:1, :]
    key_gain = gains[1:2, :]
    block = 2 * head

    def heads(step, carry):
        offset = pl.multiple_of(step * block, block)
        raw_q = dot(normed[0:half, :], weights[:, pl.ds(offset, block)])
        raw_k = dot(normed[...], weights[:, pl.ds(part + offset, block)])
        raw_v = dot(normed[...], weights[:, pl.ds(2 * part + offset, block)])
        outs = [[None] * 2 for _ in range(micro_count)]
        for i in range(2):
            cols = slice(i * head, (i + 1) * head)
            queries = unit(raw_q[:, cols], query_gain)
            keys = unit(raw_k[:, cols], key_gain)
            values = raw_v[:, cols].astype(jnp.bfloat16)
            for m in range(micro_count):
                near = slice(m * two, (m + 1) * two)
                far = slice(half + m * two, half + (m + 1) * two)
                q = queries[near]
                scale = head ** (-0.5)
                e_near = jnp.exp(dot_t(q, keys[near]) * scale) * near_masks[m]
                e_far = jnp.exp(dot_t(q, keys[far]) * scale) * far_masks[m]
                total = jnp.sum(e_near, axis=-1, keepdims=True) + jnp.sum(
                    e_far, axis=-1, keepdims=True
                )
                mixed = dot(e_near.astype(jnp.bfloat16), values[near]) + dot(
                    e_far.astype(jnp.bfloat16), values[far]
                )
                outs[m][i] = (mixed / total).astype(jnp.bfloat16)
        for m in range(micro_count):
            joined = jnp.concatenate(outs[m], axis=1)
            att_own[m, :, pl.ds(offset, block)] = joined[:view_tok]
            att_pair[m, :, pl.ds(offset, block)] = joined[view_tok:]
        return carry

    lax.fori_loop(0, part // block, heads, 0)


def project_kernel(last, *refs):
    views, att_own_src, att_got_src, stream_src, gates_src, out_weight = refs[:6]
    refs = refs[6:]
    if last:
        keep_src, refs = refs[0], refs[1:]
    result, weights, att_own, att_got, stream, gates = refs[:6]
    refs = refs[6:]
    if last:
        keep, refs = refs[0], refs[1:]
    sems, small_sems = refs
    micro_count, view_tok, part = att_own.shape
    width = out_weight.shape[1]
    place = lax.axis_index("seq")
    mine = (place + lax.axis_index("groups")) % 2
    newest = lax.axis_index("section") == lax.axis_size("section") - 1
    sets = [owner_of(views, m, place) for m in range(views.shape[0])]
    blocks = sems.shape[0]
    block = width // blocks

    def piece(index):
        return pltpu.make_async_copy(
            out_weight.at[:, pl.ds(index * block, block)],
            weights.at[:, pl.ds(index * block, block)],
            sems.at[index],
        )

    moves = [
        (att_own_src, att_own),
        (att_got_src, att_got),
        (stream_src, stream),
        (gates_src, gates),
    ]
    if last:
        moves.append((keep_src, keep))
    copies = [
        pltpu.make_async_copy(source, target, small_sems.at[i])
        for i, (source, target) in enumerate(moves)
    ]
    for copy in copies:
        copy.start()
    for index in range(blocks):
        piece(index).start()
    for copy in copies:
        copy.wait()
    tokens = micro_count * view_tok
    here = att_own[...].reshape(tokens, part)
    there = att_got[...].reshape(tokens, part)
    first = pl.multiple_of(mine * part, part)
    second = pl.multiple_of((1 - mine) * part, part)
    for index in range(blocks):
        piece(index).wait()
        cols = slice(index * block, (index + 1) * block)
        mixed = jnp.dot(
            here, weights[pl.ds(first, part), cols], preferred_element_type=jnp.float32
        ) + jnp.dot(
            there,
            weights[pl.ds(second, part), cols],
            preferred_element_type=jnp.float32,
        )
        for m in range(micro_count):
            gate = gates[sets[m]][m : m + 1, cols].astype(jnp.float32)
            value = (
                stream[m, :, cols].astype(jnp.float32)
                + gate * mixed[m * view_tok : (m + 1) * view_tok]
            ).astype(jnp.bfloat16)
            if last:
                value = jnp.where(newest, value, keep[m, :, cols])
            result[m, :, cols] = value


def tied(value, *others):
    return lax.optimization_barrier((value,) + others)[0]


def paired_body(
    stream, set_views, modulation, set_gate, qkv_weight, norm_gain, out_weight
):
    micro_count, view_tok, width = stream.shape
    head = norm_gain.shape[2]
    part = width // 2
    rows = qkv_weight.shape[1]
    seq_count = lax.axis_size("seq")
    section_count = lax.axis_size("section")
    group = lax.axis_index("groups")
    place = lax.axis_index("seq")
    core = place % 2
    chip = place // 2
    mine = core ^ group
    middle = (chip == 1) | (chip == 2)
    line_axes = ("groups", "seq")

    def along(steps):
        return [
            (g * seq_count + 2 * a + c, g * seq_count + 2 * b + c)
            for g in range(2)
            for c in range(2)
            for a, b in steps
        ]

    opposite = [
        (g * seq_count + 2 * a + c, (1 - g) * seq_count + 2 * a + 1 - c)
        for g in range(2)
        for c in range(2)
        for a in range(seq_count // 2)
    ]
    outer = along([(0, 1), (1, 0), (2, 3), (3, 2)])
    inner = along([(1, 2), (2, 1)])
    outward_steps = along([(1, 0), (2, 3)])

    def send(value, pairs):
        return lax.ppermute(value, line_axes, pairs)

    swap_cores = [(i, i ^ 1) for i in range(seq_count)]
    swap_edges = [(i, i + 1) for i in range(1, seq_count - 1, 2)] + [
        (i + 1, i) for i in range(1, seq_count - 1, 2)
    ]

    by_kind = jnp.transpose(qkv_weight[0], (1, 0, 2))
    home = [
        lax.dynamic_slice(by_kind, (kind, 0, mine * part), (1, rows, part))[0]
        for kind in range(3)
    ]
    lent = lax.dynamic_slice(by_kind, (0, 0, (1 - mine) * part), (3, rows, part))

    pair = lax.ppermute(stream, "seq", swap_cores)
    halo = lax.ppermute(stream, "seq", swap_edges)
    home_pair = lax.ppermute(lent, "seq", swap_cores)
    pair_halo = lax.ppermute(halo, "seq", swap_cores)
    first_exchange = (pair, halo, pair_halo)

    from_outer, from_inner = [], []
    across_first, inner_next, outer_next = [], [], []
    for kind in range(3):
        ready = home[kind]
        if kind == 2:
            ready = tied(ready, from_outer[0], from_inner[0])
        from_outer.append(send(ready, outer))
        from_inner.append(send(ready, inner))
    before = ()
    for kind in range(3):
        a = tied(from_outer[kind], from_inner[kind], *before)
        b = tied(from_inner[kind], from_outer[kind], *before)
        across_first.append(send(a, opposite))
        inner_next.append(send(a, inner))
        outer_next.append(send(b, outward_steps))
        before = (from_outer[kind], from_inner[kind])
    second, across_second, outer_last = [], [], []
    for kind in range(3):
        before = before + (across_first[kind],)
        a = tied(inner_next[kind], outer_next[kind], *before)
        b = tied(outer_next[kind], inner_next[kind], *before)
        outer_last.append(send(a, outward_steps))
        second.append(jnp.where(middle, from_inner[kind], b))
        across_second.append(send(second[kind], opposite))
        before = (inner_next[kind], outer_next[kind])
    third, across_third = [], []
    for kind in range(3):
        a = tied(outer_last[kind], across_second[kind], *before)
        third.append(jnp.where(middle, inner_next[kind], a))
        across_third.append(send(third[kind], opposite))
        before = (outer_last[kind],)

    pieces = (
        home
        + [home_pair[kind] for kind in range(3)]
        + from_outer
        + across_first
        + second
        + across_second
        + third
        + across_third
    )

    section_place = lax.axis_index("section")
    gates = jnp.transpose(set_gate[0], (1, 0, 2))

    vmem = pl.BlockSpec(memory_space=pltpu.VMEM)
    smem = pl.BlockSpec(memory_space=pltpu.SMEM)
    anywhere = pl.BlockSpec(memory_space=pltpu.HBM)
    half_shape = jax.ShapeDtypeStruct((micro_count, view_tok, part), jnp.bfloat16)
    attend = pl.pallas_call(
        attend_kernel,
        out_shape=(half_shape, half_shape),
        in_specs=[smem] + [anywhere] * 5 + [vmem] + [anywhere] * 24,
        out_specs=(vmem, vmem),
        scratch_shapes=[
            pltpu.VMEM((width, 3 * part), jnp.bfloat16),
            pltpu.VMEM((4 * micro_count * view_tok, width), jnp.bfloat16),
            pltpu.VMEM((4,) + stream.shape, jnp.bfloat16),
            pltpu.VMEM(modulation.shape[1:], jnp.bfloat16),
            pltpu.SemaphoreType.DMA((24,)),
            pltpu.SemaphoreType.DMA((5,)),
        ],
        compiler_params=pltpu.CompilerParams(vmem_limit_bytes=60 * 1024 * 1024),
        name="attend",
    )

    def project(last, *operands):
        spare = [pltpu.VMEM(stream.shape, jnp.bfloat16)] if last else []
        return pl.pallas_call(
            functools.partial(project_kernel, last),
            out_shape=jax.ShapeDtypeStruct(stream.shape, jnp.bfloat16),
            in_specs=[smem] + [anywhere] * (len(operands) - 1),
            out_specs=vmem,
            scratch_shapes=[
                pltpu.VMEM((width, width), jnp.bfloat16),
                pltpu.VMEM((micro_count, view_tok, part), jnp.bfloat16),
                pltpu.VMEM((micro_count, view_tok, part), jnp.bfloat16),
                pltpu.VMEM(stream.shape, jnp.bfloat16),
                pltpu.VMEM(gates.shape, jnp.bfloat16),
            ]
            + spare
            + [pltpu.SemaphoreType.DMA((3,)), pltpu.SemaphoreType.DMA((5,))],
            compiler_params=pltpu.CompilerParams(vmem_limit_bytes=60 * 1024 * 1024),
            name="project",
        )(*operands)

    own = stream
    hidden = None
    for moment in range(section_count):
        if moment > 0:
            halo = lax.ppermute(own, "seq", swap_edges)
            pair = lax.ppermute(own, "seq", swap_cores)
            pair_halo = lax.ppermute(halo, "seq", swap_cores)
        att_own, att_pair = attend(
            set_views, own, pair, halo, pair_halo, modulation[0], norm_gain[0], *pieces
        )
        att_got = lax.ppermute(att_pair, "seq", swap_cores)
        operands = (set_views, att_own, att_got, own, gates, out_weight[0])
        if moment > 0 and moment + 1 == section_count:
            hidden = project(True, *operands, hidden)
        else:
            result = project(False, *operands)
            if moment == 0:
                hidden = result
            else:
                hidden = jnp.where(section_place == moment, result, hidden)
        if moment + 1 < section_count:
            own = lax.ppermute(
                result, "section", [(i, i + 1) for i in range(section_count - 1)]
            )
    return hidden[None]


def shifted(array, axis, by):
    size = lax.axis_size(axis)
    pairs = [(i, i + by) for i in range(size) if 0 <= i + by < size]
    return lax.ppermute(array, axis, pairs)


def unit_rms(values, scaling):
    return (
        values
        * lax.rsqrt(jnp.mean(values * values, axis=-1, keepdims=True) + epsilon)
        * scaling
    )


def general_body(
    stream, set_views, modulation, set_gate, qkv_weight, norm_gain, out_weight
):
    micro_count, view_tok, local_width = stream.shape
    head_size = norm_gain.shape[2]
    head_count = local_width // head_size
    seq_count = lax.axis_size("seq")
    section_count = lax.axis_size("section")
    seq_place = lax.axis_index("seq")
    section_place = lax.axis_index("section")
    full_width = local_width * lax.axis_size("tp")
    whole_qkv = lax.all_gather(qkv_weight[0], "seq", axis=0, tiled=True)
    qkv_flat = whole_qkv.reshape(whole_qkv.shape[0], 3 * local_width)
    gain_pair = norm_gain[0]
    out_rows = out_weight[0]
    score_scale = head_size ** (-0.5)
    offsets = list(range(-REACH, REACH + 1))
    ticks = micro_count + section_count - 1
    carried = jnp.zeros((view_tok, local_width), jnp.bfloat16)
    hidden = jnp.zeros((micro_count, view_tok, local_width), jnp.bfloat16)
    for moment in range(ticks):
        fresh_input = stream[min(moment, micro_count - 1)]
        section_input = jnp.where(section_place == 0, fresh_input, carried)
        micro_raw = moment - section_place
        micro_index = jnp.clip(micro_raw, 0, micro_count - 1)
        owners = view_sets(set_views[micro_index], seq_count)
        own_set = owners[seq_place]
        widened = section_input.astype(jnp.float32)
        totals, squares = lax.psum(
            (jnp.sum(widened, axis=1), jnp.sum(widened * widened, axis=1)), "tp"
        )
        average = (totals / full_width)[:, None]
        spread = (squares / full_width)[:, None] - average * average
        factors = modulation[0, micro_index, own_set].astype(jnp.float32)
        normed = (
            (widened - average) * lax.rsqrt(spread + epsilon) * (1.0 + factors[1])
            + factors[0]
        ).astype(jnp.bfloat16)
        projected = jnp.dot(
            lax.all_gather(normed, "tp", axis=1, tiled=True),
            qkv_flat,
            preferred_element_type=jnp.float32,
        )
        parts = projected.reshape(view_tok, 3, head_count, head_size)
        queries = unit_rms(parts[:, 0], gain_pair[0]).astype(jnp.bfloat16)
        keys_here = unit_rms(parts[:, 1], gain_pair[1]).astype(jnp.bfloat16)
        values_here = parts[:, 2].astype(jnp.bfloat16)
        payload = jnp.stack(
            [
                keys_here.reshape(view_tok, local_width),
                values_here.reshape(view_tok, local_width),
            ]
        )
        arrived = [shifted(payload, "seq", 1), payload, shifted(payload, "seq", -1)]
        key_list = [r[0].reshape(view_tok, head_count, head_size) for r in arrived]
        value_list = [r[1].reshape(view_tok, head_count, head_size) for r in arrived]
        visible = []
        for offset in offsets:
            neighbour = seq_place + offset
            in_range = (neighbour >= 0) & (neighbour < seq_count)
            same_set = owners[jnp.clip(neighbour, 0, seq_count - 1)] == own_set
            visible.append((in_range & same_set).astype(jnp.float32))
        keys_cat = jnp.concatenate(key_list, axis=0)
        values_cat = jnp.concatenate(value_list, axis=0)
        mask_row = jnp.repeat(jnp.stack(visible), view_tok)
        scores = (
            jnp.einsum(
                "qhd,khd->hqk", queries, keys_cat, preferred_element_type=jnp.float32
            )
            * score_scale
        )
        exponent = jnp.exp(scores) * mask_row
        denominator = jnp.sum(exponent, axis=-1)
        numerator = jnp.einsum(
            "hqk,khd->qhd",
            exponent.astype(jnp.bfloat16),
            values_cat,
            preferred_element_type=jnp.float32,
        )
        attended = (
            (numerator / jnp.transpose(denominator)[:, :, None])
            .astype(jnp.bfloat16)
            .reshape(view_tok, local_width)
        )
        mixed_out = jnp.dot(
            lax.all_gather(attended, "tp", axis=1, tiled=True),
            out_rows,
            preferred_element_type=jnp.float32,
        )
        gating = set_gate[0, micro_index, own_set].astype(jnp.float32)
        result = (widened + gating * mixed_out).astype(jnp.bfloat16)
        in_range = (micro_raw >= 0) & (micro_raw < micro_count)
        hidden = jnp.where(in_range, hidden.at[micro_index].set(result), hidden)
        if moment + 1 < ticks:
            carried = shifted(result, "section", 1)
    return hidden[None]


def solution(mesh):
    placed = (
        P("groups", "seq", "tp"),
        P("groups", None),
        P("section", "groups", None, None, "tp"),
        P("section", "groups", None, "tp"),
        P("section", "seq", None, "tp"),
        P("section", None, None),
        P("section", None, "tp"),
    )
    sizes = mesh.shape
    paired = sizes["tp"] == 1 and sizes["groups"] == 2 and sizes["seq"] == 8
    return jax.shard_map(
        paired_body if paired else general_body,
        mesh=mesh,
        in_specs=placed,
        out_specs=P("section", "groups", "seq", "tp"),
        check_vma=False,
    )
```

```python
import functools

import jax
import jax.numpy as jnp
from jax import lax
from jax.experimental import pallas as pl
from jax.experimental.pallas import tpu as pltpu
from jax.sharding import PartitionSpec as P

REACH = 1


epsilon = 1e-06


def view_sets(set_views, count):
    amount = set_views.shape[0]
    before = jnp.arange(amount)[:, None] > jnp.arange(amount)[None, :]
    starts = jnp.sum(jnp.where(before, set_views[None, :], 0), axis=1)
    position = jnp.arange(count, dtype=jnp.int32)
    inside = (starts[None, :] <= position[:, None]).astype(jnp.int32)
    return jnp.sum(inside, axis=1) - 1


def owner_of(views, m, place):
    start, owner = jnp.int32(0), jnp.int32(-1)
    for j in range(views.shape[1]):
        owner = owner + jnp.where(start <= place, 1, 0)
        start = start + views[m, j]
    return owner


def attend_table(views):
    count = lax.axis_size("seq")
    place = lax.axis_index("seq")
    core = place % 2
    chip = place // 2
    middle = (chip == 1) | (chip == 2)
    others = (
        chip,
        chip + 1 - 2 * (chip % 2),
        jnp.where(middle, 3 - chip, (chip + 2) % 4),
        jnp.where(middle, jnp.where(chip == 1, 3, 0), 3 - chip),
    )
    order = []
    for other in others:
        order += [2 * other + core, 2 * other + 1 - core]
    outward = 2 * core - 1
    pair_place = place - outward
    halo_place = place + outward
    pair_halo_place = pair_place - outward
    places = (place, pair_place, halo_place, pair_halo_place)
    sets, masks = [], []
    for m in range(views.shape[0]):
        found = [
            owner_of(views, m, jnp.clip(where, 0, count - 1)) for where in places
        ]
        sets.append(found)
        masks.append(
            (
                found[0] == found[1],
                (halo_place >= 0) & (halo_place < count) & (found[0] == found[2]),
                (pair_halo_place >= 0)
                & (pair_halo_place < count)
                & (found[1] == found[3]),
            )
        )
    return order, sets, masks


def normalise(source, m, slot, modulation, sets, normed, dtype=jnp.bfloat16):
    micro_count, view_tok, _ = source.shape
    wide = source[m].astype(jnp.float32)
    average = jnp.mean(wide, axis=-1, keepdims=True)
    squares = jnp.mean(wide * wide, axis=-1, keepdims=True)
    spread = squares - average * average
    factors = modulation[m, sets[m][slot]].astype(jnp.float32)
    value = (wide - average) * lax.rsqrt(spread + epsilon) * (
        1.0 + factors[1:2]
    ) + factors[0:1]
    half = 2 * micro_count * view_tok
    first = half * (slot // 2) + (2 * m + slot % 2) * view_tok
    normed[first : first + view_tok, :] = value.astype(dtype)


def norm_kernel(views, own, pair, halo, pair_halo, modulation, normed):
    _, sets, _ = attend_table(views)
    for slot, source in enumerate((own, pair, halo, pair_halo)):
        for m in range(source.shape[0]):
            normalise(source, m, slot, modulation, sets, normed)


def set_masks(masks, view_tok):
    two = 2 * view_tok
    low_row = lax.broadcasted_iota(jnp.int32, (two, two), 0) < view_tok
    low_col = lax.broadcasted_iota(jnp.int32, (two, two), 1) < view_tok
    near_masks, far_masks = [], []
    for found in masks:
        together, below, above = (jnp.where(mask, 1.0, 0.0) for mask in found)
        near_masks.append(jnp.where(low_row == low_col, 1.0, together))
        far_masks.append(
            jnp.where(
                low_row & low_col,
                below,
                jnp.where(low_row | low_col, 0.0, above),
            )
        )
    return near_masks, far_masks


def attend_heads(normed, weights, gains, near_masks, far_masks, view_tok, outputs):
    micro_count = len(near_masks)
    part = weights.shape[1] // 3
    head = gains.shape[1]
    two = 2 * view_tok
    half = micro_count * two

    def unit(values, gain):
        return (
            values
            * lax.rsqrt(jnp.mean(values * values, axis=-1, keepdims=True) + epsilon)
            * gain
        ).astype(jnp.bfloat16)

    def dot(a, b):
        return jnp.dot(a, b, preferred_element_type=jnp.float32)

    def dot_t(a, b):
        return lax.dot_general(
            a, b, (((1,), (1,)), ((), ())), preferred_element_type=jnp.float32
        )

    raw_q = dot(normed[0:half, :], weights[:, 0:part])
    raw_k = dot(normed[...], weights[:, part : 2 * part])
    raw_v = dot(normed[...], weights[:, 2 * part : 3 * part])
    count = part // head
    outs = [[None] * count for _ in range(micro_count)]
    for i in range(count):
        cols = slice(i * head, (i + 1) * head)
        queries = unit(raw_q[:, cols], gains[0:1, :])
        keys = unit(raw_k[:, cols], gains[1:2, :])
        values = raw_v[:, cols].astype(jnp.bfloat16)
        for m in range(micro_count):
            near = slice(m * two, (m + 1) * two)
            far = slice(half + m * two, half + (m + 1) * two)
            q = queries[near]
            scale = head ** (-0.5)
            e_near = jnp.exp(dot_t(q, keys[near]) * scale) * near_masks[m]
            e_far = jnp.exp(dot_t(q, keys[far]) * scale) * far_masks[m]
            total = jnp.sum(e_near, axis=-1, keepdims=True) + jnp.sum(
                e_far, axis=-1, keepdims=True
            )
            mixed = dot(e_near.astype(jnp.bfloat16), values[near]) + dot(
                e_far.astype(jnp.bfloat16), values[far]
            )
            outs[m][i] = (mixed / total).astype(jnp.bfloat16)
    att_own, att_pair, offset = outputs
    for m in range(micro_count):
        joined = jnp.concatenate(outs[m], axis=1)
        att_own[m, :, offset : offset + part] = joined[:view_tok]
        att_pair[m, :, offset : offset + part] = joined[view_tok:]


def attend_part_kernel(index, *refs):
    views, normed, gains = refs[:3]
    pieces = refs[3:11]
    att_own, att_pair, weights, sems = refs[-4:]
    rows, part = pieces[0].shape[1:]
    view_tok = att_own.shape[1]
    order, _, masks = attend_table(views)
    moves = []
    for slot in range(8):
        start = pl.multiple_of(order[slot] * rows, rows)
        for kind in range(3):
            moves.append(
                pltpu.make_async_copy(
                    pieces[slot].at[kind],
                    weights.at[pl.ds(start, rows), pl.ds(kind * part, part)],
                    sems.at[3 * slot + kind],
                )
            )
    for move in moves:
        move.start()
    near_masks, far_masks = set_masks(masks, view_tok)
    for move in moves:
        move.wait()
    attend_heads(
        normed,
        weights,
        gains,
        near_masks,
        far_masks,
        view_tok,
        (att_own, att_pair, index * part),
    )


def attend_kernel(*refs):
    views, own, pair, halo, pair_halo, modulation, gains = refs[:7]
    weights = refs[7:10]
    att_own, att_pair, normed, streams, sems = refs[10:]
    micro_count, view_tok, _ = own.shape
    _, sets, masks = attend_table(views)
    incoming = [
        pltpu.make_async_copy(source, streams.at[slot], sems.at[slot])
        for slot, source in enumerate((own, pair, halo, pair_halo))
    ]
    for move in incoming:
        move.start()
    near_masks, far_masks = set_masks(masks, view_tok)
    for slot in range(4):
        incoming[slot].wait()
        for m in range(micro_count):
            normalise(streams.at[slot], m, slot, modulation, sets, normed)
    part = weights[0].shape[1] // 3
    for index in range(3):
        attend_heads(
            normed,
            weights[index],
            gains,
            near_masks,
            far_masks,
            view_tok,
            (att_own, att_pair, index * part),
        )


def project_kernel(last, *refs):
    views, att_own_src, att_got_src, stream_src, gates_src, out_weight = refs[:6]
    refs = refs[6:]
    if last:
        keep_src, refs = refs[0], refs[1:]
    result, att_own, att_got, stream, gates = refs[:5]
    refs = refs[5:]
    if last:
        keep, refs = refs[0], refs[1:]
    (small_sems,) = refs
    micro_count, view_tok, part = att_own.shape
    width = out_weight.shape[1]
    place = lax.axis_index("seq")
    mine = (place + lax.axis_index("groups")) % 2
    newest = lax.axis_index("section") == lax.axis_size("section") - 1
    sets = [owner_of(views, m, place) for m in range(views.shape[0])]
    blocks = 3
    block = width // blocks

    moves = [
        (att_own_src, att_own),
        (att_got_src, att_got),
        (stream_src, stream),
        (gates_src, gates),
    ]
    if last:
        moves.append((keep_src, keep))
    copies = [
        pltpu.make_async_copy(source, target, small_sems.at[i])
        for i, (source, target) in enumerate(moves)
    ]
    for copy in copies:
        copy.start()
    for copy in copies:
        copy.wait()
    tokens = micro_count * view_tok
    here = att_own[...].reshape(tokens, part)
    there = att_got[...].reshape(tokens, part)
    first = pl.multiple_of(mine * part, part)
    second = pl.multiple_of((1 - mine) * part, part)
    for index in range(blocks):
        cols = slice(index * block, (index + 1) * block)
        mixed = jnp.dot(
            here, out_weight[pl.ds(first, part), cols], preferred_element_type=jnp.float32
        ) + jnp.dot(
            there,
            out_weight[pl.ds(second, part), cols],
            preferred_element_type=jnp.float32,
        )
        for m in range(micro_count):
            gate = gates[sets[m]][m : m + 1, cols].astype(jnp.float32)
            value = (
                stream[m, :, cols].astype(jnp.float32)
                + gate * mixed[m * view_tok : (m + 1) * view_tok]
            ).astype(jnp.bfloat16)
            if last:
                value = jnp.where(newest, value, keep[m, :, cols])
            result[m, :, cols] = value


def tied(value, *others):
    return lax.optimization_barrier((value,) + others)[0]


def paired_body(
    stream, set_views, modulation, set_gate, qkv_weight, norm_gain, out_weight
):
    micro_count, view_tok, width = stream.shape
    head = norm_gain.shape[2]
    part = width // 2
    rows = qkv_weight.shape[1]
    seq_count = lax.axis_size("seq")
    section_count = lax.axis_size("section")
    group = lax.axis_index("groups")
    place = lax.axis_index("seq")
    core = place % 2
    chip = place // 2
    mine = core ^ group
    middle = (chip == 1) | (chip == 2)
    line_axes = ("groups", "seq")

    def along(steps):
        return [
            (g * seq_count + 2 * a + c, g * seq_count + 2 * b + c)
            for g in range(2)
            for c in range(2)
            for a, b in steps
        ]

    opposite = [
        (g * seq_count + 2 * a + c, (1 - g) * seq_count + 2 * a + 1 - c)
        for g in range(2)
        for c in range(2)
        for a in range(seq_count // 2)
    ]
    outer = along([(0, 1), (1, 0), (2, 3), (3, 2)])
    inner = along([(1, 2), (2, 1)])
    outward_steps = along([(1, 0), (2, 3)])

    def send(value, pairs):
        return lax.ppermute(value, line_axes, pairs)

    swap_cores = [(i, i ^ 1) for i in range(seq_count)]
    swap_edges = [(i, i + 1) for i in range(1, seq_count - 1, 2)] + [
        (i + 1, i) for i in range(1, seq_count - 1, 2)
    ]

    by_kind = jnp.transpose(qkv_weight[0], (1, 0, 2))
    third_part = part // 3

    def columns(which, index):
        return lax.dynamic_slice(
            by_kind, (0, 0, which * part + index * third_part), (3, rows, third_part)
        )

    home = [columns(mine, index) for index in range(3)]
    lent = [columns(1 - mine, index) for index in range(3)]

    pair = lax.ppermute(stream, "seq", swap_cores)
    halo = lax.ppermute(stream, "seq", swap_edges)
    home_pair = lax.ppermute(jnp.stack(lent), "seq", swap_cores)
    pair_halo = lax.ppermute(halo, "seq", swap_cores)
    first_exchange = (pair, halo, pair_halo)

    from_outer, from_inner = [], []
    across_first, inner_next, outer_next = [], [], []
    for kind in range(3):
        ready = home[kind]
        if kind == 2:
            ready = tied(ready, from_outer[0], from_inner[0])
        from_outer.append(send(ready, outer))
        from_inner.append(send(ready, inner))
    before = ()
    for kind in range(3):
        a = tied(from_outer[kind], from_inner[kind], *before)
        b = tied(from_inner[kind], from_outer[kind], *before)
        across_first.append(send(a, opposite))
        inner_next.append(send(a, inner))
        outer_next.append(send(b, outward_steps))
        before = (from_outer[kind], from_inner[kind])
    second, across_second, outer_last = [], [], []
    for kind in range(3):
        before = before + (across_first[kind],)
        a = tied(inner_next[kind], outer_next[kind], *before)
        b = tied(outer_next[kind], inner_next[kind], *before)
        outer_last.append(send(a, outward_steps))
        second.append(jnp.where(middle, from_inner[kind], b))
        across_second.append(send(second[kind], opposite))
        before = (inner_next[kind], outer_next[kind])
    third, across_third = [], []
    for kind in range(3):
        a = tied(outer_last[kind], across_second[kind], *before)
        third.append(jnp.where(middle, inner_next[kind], a))
        across_third.append(send(third[kind], opposite))
        before = (outer_last[kind],)

    section_place = lax.axis_index("section")
    gates = jnp.transpose(set_gate[0], (1, 0, 2))

    vmem = pl.BlockSpec(memory_space=pltpu.VMEM)
    smem = pl.BlockSpec(memory_space=pltpu.SMEM)
    anywhere = pl.BlockSpec(memory_space=pl.ANY)
    half_shape = jax.ShapeDtypeStruct((micro_count, view_tok, part), jnp.bfloat16)
    normed_shape = (4 * micro_count * view_tok, width)
    mega = 1024 * 1024

    def limit(size):
        return pltpu.CompilerParams(vmem_limit_bytes=size * mega)

    norm = pl.pallas_call(
        norm_kernel,
        out_shape=jax.ShapeDtypeStruct(normed_shape, jnp.bfloat16),
        in_specs=[smem] + [vmem] * 5,
        out_specs=vmem,
        compiler_params=limit(12),
        name="norm",
    )

    def attend_part(index, normed, pieces, earlier):
        return pl.pallas_call(
            functools.partial(attend_part_kernel, index),
            out_shape=(
                half_shape,
                half_shape,
                jax.ShapeDtypeStruct((width, part), jnp.bfloat16),
            ),
            in_specs=[smem, vmem, vmem] + [anywhere] * 8 + [vmem] * len(earlier),
            out_specs=(vmem, vmem, vmem),
            scratch_shapes=[pltpu.SemaphoreType.DMA((24,))],
            input_output_aliases={11: 0, 12: 1} if earlier else {},
            compiler_params=limit(20),
            name="attend_part",
        )(set_views, normed, norm_gain[0], *pieces, *earlier)

    attend = pl.pallas_call(
        attend_kernel,
        out_shape=(half_shape, half_shape),
        in_specs=[smem] + [anywhere] * 4 + [vmem] * 5,
        out_specs=(vmem, vmem),
        scratch_shapes=[
            pltpu.VMEM(normed_shape, jnp.bfloat16),
            pltpu.VMEM((4,) + stream.shape, jnp.bfloat16),
            pltpu.SemaphoreType.DMA((4,)),
        ],
        compiler_params=limit(24),
        name="attend",
    )

    def project(last, *operands):
        spare = [pltpu.VMEM(stream.shape, jnp.bfloat16)] if last else []
        in_specs = [smem] + [anywhere] * 4 + [vmem] + [anywhere] * last
        return pl.pallas_call(
            functools.partial(project_kernel, last),
            out_shape=jax.ShapeDtypeStruct(stream.shape, jnp.bfloat16),
            in_specs=in_specs,
            out_specs=vmem,
            scratch_shapes=[
                pltpu.VMEM((micro_count, view_tok, part), jnp.bfloat16),
                pltpu.VMEM((micro_count, view_tok, part), jnp.bfloat16),
                pltpu.VMEM(stream.shape, jnp.bfloat16),
                pltpu.VMEM(gates.shape, jnp.bfloat16),
            ]
            + spare
            + [pltpu.SemaphoreType.DMA((5,))],
            compiler_params=limit(12),
            name="project",
        )(*operands)

    own = stream
    hidden = None
    for moment in range(section_count):
        if moment > 0:
            halo = lax.ppermute(own, "seq", swap_edges)
            pair = lax.ppermute(own, "seq", swap_cores)
            pair_halo = lax.ppermute(halo, "seq", swap_cores)
            att_own, att_pair = attend(
                set_views,
                own,
                pair,
                halo,
                pair_halo,
                modulation[0],
                norm_gain[0],
                *assembled,
            )
        else:
            normed = norm(set_views, own, pair, halo, pair_halo, modulation[0])
            earlier, assembled = (), []
            for index in range(3):
                pieces = [
                    home[index],
                    home_pair[index],
                    from_outer[index],
                    across_first[index],
                    second[index],
                    across_second[index],
                    third[index],
                    across_third[index],
                ]
                *earlier, joined = attend_part(index, normed, pieces, earlier)
                assembled.append(joined)
            att_own, att_pair = earlier
        att_got = lax.ppermute(att_pair, "seq", swap_cores)
        operands = (set_views, att_own, att_got, own, gates, out_weight[0])
        if moment > 0 and moment + 1 == section_count:
            hidden = project(True, *operands, hidden)
        else:
            result = project(False, *operands)
            if moment == 0:
                hidden = result
            else:
                hidden = jnp.where(section_place == moment, result, hidden)
        if moment + 1 < section_count:
            own = lax.ppermute(
                result, "section", [(i, i + 1) for i in range(section_count - 1)]
            )
    return hidden[None]


def shifted(array, axis, by):
    size = lax.axis_size(axis)
    pairs = [(i, i + by) for i in range(size) if 0 <= i + by < size]
    return lax.ppermute(array, axis, pairs)


def unit_rms(values, scaling):
    return (
        values
        * lax.rsqrt(jnp.mean(values * values, axis=-1, keepdims=True) + epsilon)
        * scaling
    )


def general_body(
    stream, set_views, modulation, set_gate, qkv_weight, norm_gain, out_weight
):
    micro_count, view_tok, local_width = stream.shape
    head_size = norm_gain.shape[2]
    head_count = local_width // head_size
    seq_count = lax.axis_size("seq")
    section_count = lax.axis_size("section")
    seq_place = lax.axis_index("seq")
    section_place = lax.axis_index("section")
    full_width = local_width * lax.axis_size("tp")
    whole_qkv = lax.all_gather(qkv_weight[0], "seq", axis=0, tiled=True)
    qkv_flat = whole_qkv.reshape(whole_qkv.shape[0], 3 * local_width)
    gain_pair = norm_gain[0]
    out_rows = out_weight[0]
    score_scale = head_size ** (-0.5)
    offsets = list(range(-REACH, REACH + 1))
    ticks = micro_count + section_count - 1
    carried = jnp.zeros((view_tok, local_width), jnp.bfloat16)
    hidden = jnp.zeros((micro_count, view_tok, local_width), jnp.bfloat16)
    for moment in range(ticks):
        fresh_input = stream[min(moment, micro_count - 1)]
        section_input = jnp.where(section_place == 0, fresh_input, carried)
        micro_raw = moment - section_place
        micro_index = jnp.clip(micro_raw, 0, micro_count - 1)
        owners = view_sets(set_views[micro_index], seq_count)
        own_set = owners[seq_place]
        widened = section_input.astype(jnp.float32)
        totals, squares = lax.psum(
            (jnp.sum(widened, axis=1), jnp.sum(widened * widened, axis=1)), "tp"
        )
        average = (totals / full_width)[:, None]
        spread = (squares / full_width)[:, None] - average * average
        factors = modulation[0, micro_index, own_set].astype(jnp.float32)
        normed = (
            (widened - average) * lax.rsqrt(spread + epsilon) * (1.0 + factors[1])
            + factors[0]
        ).astype(jnp.bfloat16)
        projected = jnp.dot(
            lax.all_gather(normed, "tp", axis=1, tiled=True),
            qkv_flat,
            preferred_element_type=jnp.float32,
        )
        parts = projected.reshape(view_tok, 3, head_count, head_size)
        queries = unit_rms(parts[:, 0], gain_pair[0]).astype(jnp.bfloat16)
        keys_here = unit_rms(parts[:, 1], gain_pair[1]).astype(jnp.bfloat16)
        values_here = parts[:, 2].astype(jnp.bfloat16)
        payload = jnp.stack(
            [
                keys_here.reshape(view_tok, local_width),
                values_here.reshape(view_tok, local_width),
            ]
        )
        arrived = [shifted(payload, "seq", 1), payload, shifted(payload, "seq", -1)]
        key_list = [r[0].reshape(view_tok, head_count, head_size) for r in arrived]
        value_list = [r[1].reshape(view_tok, head_count, head_size) for r in arrived]
        visible = []
        for offset in offsets:
            neighbour = seq_place + offset
            in_range = (neighbour >= 0) & (neighbour < seq_count)
            same_set = owners[jnp.clip(neighbour, 0, seq_count - 1)] == own_set
            visible.append((in_range & same_set).astype(jnp.float32))
        keys_cat = jnp.concatenate(key_list, axis=0)
        values_cat = jnp.concatenate(value_list, axis=0)
        mask_row = jnp.repeat(jnp.stack(visible), view_tok)
        scores = (
            jnp.einsum(
                "qhd,khd->hqk", queries, keys_cat, preferred_element_type=jnp.float32
            )
            * score_scale
        )
        exponent = jnp.exp(scores) * mask_row
        denominator = jnp.sum(exponent, axis=-1)
        numerator = jnp.einsum(
            "hqk,khd->qhd",
            exponent.astype(jnp.bfloat16),
            values_cat,
            preferred_element_type=jnp.float32,
        )
        attended = (
            (numerator / jnp.transpose(denominator)[:, :, None])
            .astype(jnp.bfloat16)
            .reshape(view_tok, local_width)
        )
        mixed_out = jnp.dot(
            lax.all_gather(attended, "tp", axis=1, tiled=True),
            out_rows,
            preferred_element_type=jnp.float32,
        )
        gating = set_gate[0, micro_index, own_set].astype(jnp.float32)
        result = (widened + gating * mixed_out).astype(jnp.bfloat16)
        in_range = (micro_raw >= 0) & (micro_raw < micro_count)
        hidden = jnp.where(in_range, hidden.at[micro_index].set(result), hidden)
        if moment + 1 < ticks:
            carried = shifted(result, "section", 1)
    return hidden[None]


def solution(mesh):
    placed = (
        P("groups", "seq", "tp"),
        P("groups", None),
        P("section", "groups", None, None, "tp"),
        P("section", "groups", None, "tp"),
        P("section", "seq", None, "tp"),
        P("section", None, None),
        P("section", None, "tp"),
    )
    sizes = mesh.shape
    paired = sizes["tp"] == 1 and sizes["groups"] == 2 and sizes["seq"] == 8
    return jax.shard_map(
        paired_body if paired else general_body,
        mesh=mesh,
        in_specs=placed,
        out_specs=P("section", "groups", "seq", "tp"),
        check_vma=False,
    )
```

```python
import functools

import jax
import jax.numpy as jnp
from jax import lax
from jax.experimental import pallas as pl
from jax.experimental.pallas import tpu as pltpu
from jax.sharding import PartitionSpec as P

REACH = 1


epsilon = 1e-06


def view_sets(set_views, count):
    amount = set_views.shape[0]
    before = jnp.arange(amount)[:, None] > jnp.arange(amount)[None, :]
    starts = jnp.sum(jnp.where(before, set_views[None, :], 0), axis=1)
    position = jnp.arange(count, dtype=jnp.int32)
    inside = (starts[None, :] <= position[:, None]).astype(jnp.int32)
    return jnp.sum(inside, axis=1) - 1


def owner_of(views, m, place):
    start, owner = jnp.int32(0), jnp.int32(-1)
    for j in range(views.shape[1]):
        owner = owner + jnp.where(start <= place, 1, 0)
        start = start + views[m, j]
    return owner


def attend_table(views):
    count = lax.axis_size("seq")
    place = lax.axis_index("seq")
    core = place % 2
    chip = place // 2
    middle = (chip == 1) | (chip == 2)
    others = (
        chip,
        chip + 1 - 2 * (chip % 2),
        jnp.where(middle, 3 - chip, (chip + 2) % 4),
        jnp.where(middle, jnp.where(chip == 1, 3, 0), 3 - chip),
    )
    order = []
    for other in others:
        order += [2 * other + core, 2 * other + 1 - core]
    outward = 2 * core - 1
    pair_place = place - outward
    halo_place = place + outward
    pair_halo_place = pair_place - outward
    places = (place, pair_place, halo_place, pair_halo_place)
    sets, masks = [], []
    for m in range(views.shape[0]):
        found = [
            owner_of(views, m, jnp.clip(where, 0, count - 1)) for where in places
        ]
        sets.append(found)
        masks.append(
            (
                found[0] == found[1],
                (halo_place >= 0) & (halo_place < count) & (found[0] == found[2]),
                (pair_halo_place >= 0)
                & (pair_halo_place < count)
                & (found[1] == found[3]),
            )
        )
    return order, sets, masks


def normalise(source, m, slot, modulation, sets, normed, dtype=jnp.bfloat16):
    micro_count, view_tok, _ = source.shape
    wide = source[m].astype(jnp.float32)
    average = jnp.mean(wide, axis=-1, keepdims=True)
    squares = jnp.mean(wide * wide, axis=-1, keepdims=True)
    spread = squares - average * average
    factors = modulation[m, sets[m][slot]].astype(jnp.float32)
    value = (wide - average) * lax.rsqrt(spread + epsilon) * (
        1.0 + factors[1:2]
    ) + factors[0:1]
    half = 2 * micro_count * view_tok
    first = half * (slot // 2) + (2 * m + slot % 2) * view_tok
    normed[first : first + view_tok, :] = value.astype(dtype)


def norm_kernel(views, own, pair, halo, pair_halo, modulation, normed):
    _, sets, _ = attend_table(views)
    for slot, source in enumerate((own, pair, halo, pair_halo)):
        for m in range(source.shape[0]):
            normalise(source, m, slot, modulation, sets, normed)


def set_masks(masks, view_tok):
    two = 2 * view_tok
    low_row = lax.broadcasted_iota(jnp.int32, (two, two), 0) < view_tok
    low_col = lax.broadcasted_iota(jnp.int32, (two, two), 1) < view_tok
    near_masks, far_masks = [], []
    for found in masks:
        together, below, above = (jnp.where(mask, 1.0, 0.0) for mask in found)
        near_masks.append(jnp.where(low_row == low_col, 1.0, together))
        far_masks.append(
            jnp.where(
                low_row & low_col,
                below,
                jnp.where(low_row | low_col, 0.0, above),
            )
        )
    return near_masks, far_masks


def attend_heads(normed, weights, gains, near_masks, far_masks, view_tok, outputs):
    micro_count = len(near_masks)
    part = weights.shape[1] // 3
    head = gains.shape[1]
    two = 2 * view_tok
    half = micro_count * two

    def unit(values, gain):
        return (
            values
            * lax.rsqrt(jnp.mean(values * values, axis=-1, keepdims=True) + epsilon)
            * gain
        ).astype(jnp.bfloat16)

    def dot(a, b):
        return jnp.dot(a, b, preferred_element_type=jnp.float32)

    def dot_t(a, b):
        return lax.dot_general(
            a, b, (((1,), (1,)), ((), ())), preferred_element_type=jnp.float32
        )

    raw_q = dot(normed[0:half, :], weights[:, 0:part])
    raw_k = dot(normed[...], weights[:, part : 2 * part])
    raw_v = dot(normed[...], weights[:, 2 * part : 3 * part])
    count = part // head
    outs = [[None] * count for _ in range(micro_count)]
    for i in range(count):
        cols = slice(i * head, (i + 1) * head)
        queries = unit(raw_q[:, cols], gains[0:1, :])
        keys = unit(raw_k[:, cols], gains[1:2, :])
        values = raw_v[:, cols].astype(jnp.bfloat16)
        for m in range(micro_count):
            near = slice(m * two, (m + 1) * two)
            far = slice(half + m * two, half + (m + 1) * two)
            q = queries[near]
            scale = head ** (-0.5)
            e_near = jnp.exp(dot_t(q, keys[near]) * scale) * near_masks[m]
            e_far = jnp.exp(dot_t(q, keys[far]) * scale) * far_masks[m]
            total = jnp.sum(e_near, axis=-1, keepdims=True) + jnp.sum(
                e_far, axis=-1, keepdims=True
            )
            mixed = dot(e_near.astype(jnp.bfloat16), values[near]) + dot(
                e_far.astype(jnp.bfloat16), values[far]
            )
            outs[m][i] = (mixed / total).astype(jnp.bfloat16)
    att_own, att_pair, offset = outputs
    for m in range(micro_count):
        joined = jnp.concatenate(outs[m], axis=1)
        att_own[m, :, offset : offset + part] = joined[:view_tok]
        att_pair[m, :, offset : offset + part] = joined[view_tok:]


def attend_part_kernel(offset, *refs):
    views, normed, gains = refs[:3]
    pieces = refs[3:11]
    att_own, att_pair, weights, sems = refs[-4:]
    rows, part = pieces[0].shape[1:]
    view_tok = att_own.shape[1]
    order, _, masks = attend_table(views)
    moves = []
    for slot in range(8):
        start = pl.multiple_of(order[slot] * rows, rows)
        for kind in range(3):
            source = pieces[slot].at[kind]
            if slot == 1:
                source = source.at[:, pl.ds(offset, part)]
            moves.append(
                pltpu.make_async_copy(
                    source,
                    weights.at[pl.ds(start, rows), pl.ds(kind * part, part)],
                    sems.at[3 * slot + kind],
                )
            )
    for move in moves:
        move.start()
    near_masks, far_masks = set_masks(masks, view_tok)
    for move in moves:
        move.wait()
    attend_heads(
        normed,
        weights,
        gains,
        near_masks,
        far_masks,
        view_tok,
        (att_own, att_pair, offset),
    )


def attend_kernel(*refs):
    views, own, pair, halo, pair_halo, modulation, gains = refs[:7]
    weights = refs[7:10]
    att_own, att_pair, normed, streams, sems = refs[10:]
    micro_count, view_tok, _ = own.shape
    _, sets, masks = attend_table(views)
    incoming = [
        pltpu.make_async_copy(source, streams.at[slot], sems.at[slot])
        for slot, source in enumerate((own, pair, halo, pair_halo))
    ]
    for move in incoming:
        move.start()
    near_masks, far_masks = set_masks(masks, view_tok)
    for slot in range(4):
        incoming[slot].wait()
        for m in range(micro_count):
            normalise(streams.at[slot], m, slot, modulation, sets, normed)
    offset = 0
    for index in range(3):
        attend_heads(
            normed,
            weights[index],
            gains,
            near_masks,
            far_masks,
            view_tok,
            (att_own, att_pair, offset),
        )
        offset += weights[index].shape[1] // 3


def project_kernel(last, *refs):
    views, att_own_src, att_got_src, stream_src, gates_src, out_weight = refs[:6]
    refs = refs[6:]
    if last:
        keep_src, refs = refs[0], refs[1:]
    result, att_own, att_got, stream, gates = refs[:5]
    refs = refs[5:]
    if last:
        keep, refs = refs[0], refs[1:]
    (small_sems,) = refs
    micro_count, view_tok, part = att_own.shape
    width = out_weight.shape[1]
    place = lax.axis_index("seq")
    mine = (place + lax.axis_index("groups")) % 2
    newest = lax.axis_index("section") == lax.axis_size("section") - 1
    sets = [owner_of(views, m, place) for m in range(views.shape[0])]
    blocks = 3
    block = width // blocks

    moves = [
        (att_own_src, att_own),
        (att_got_src, att_got),
        (stream_src, stream),
        (gates_src, gates),
    ]
    if last:
        moves.append((keep_src, keep))
    copies = [
        pltpu.make_async_copy(source, target, small_sems.at[i])
        for i, (source, target) in enumerate(moves)
    ]
    for copy in copies:
        copy.start()
    for copy in copies:
        copy.wait()
    tokens = micro_count * view_tok
    here = att_own[...].reshape(tokens, part)
    there = att_got[...].reshape(tokens, part)
    first = pl.multiple_of(mine * part, part)
    second = pl.multiple_of((1 - mine) * part, part)
    for index in range(blocks):
        cols = slice(index * block, (index + 1) * block)
        mixed = jnp.dot(
            here, out_weight[pl.ds(first, part), cols], preferred_element_type=jnp.float32
        ) + jnp.dot(
            there,
            out_weight[pl.ds(second, part), cols],
            preferred_element_type=jnp.float32,
        )
        for m in range(micro_count):
            gate = gates[sets[m]][m : m + 1, cols].astype(jnp.float32)
            value = (
                stream[m, :, cols].astype(jnp.float32)
                + gate * mixed[m * view_tok : (m + 1) * view_tok]
            ).astype(jnp.bfloat16)
            if last:
                value = jnp.where(newest, value, keep[m, :, cols])
            result[m, :, cols] = value


def tied(value, *others):
    return lax.optimization_barrier((value,) + others)[0]


def paired_body(
    stream, set_views, modulation, set_gate, qkv_weight, norm_gain, out_weight
):
    micro_count, view_tok, width = stream.shape
    head = norm_gain.shape[2]
    part = width // 2
    rows = qkv_weight.shape[1]
    seq_count = lax.axis_size("seq")
    section_count = lax.axis_size("section")
    group = lax.axis_index("groups")
    place = lax.axis_index("seq")
    core = place % 2
    chip = place // 2
    mine = core ^ group
    middle = (chip == 1) | (chip == 2)
    line_axes = ("groups", "seq")

    def along(steps):
        return [
            (g * seq_count + 2 * a + c, g * seq_count + 2 * b + c)
            for g in range(2)
            for c in range(2)
            for a, b in steps
        ]

    opposite = [
        (g * seq_count + 2 * a + c, (1 - g) * seq_count + 2 * a + 1 - c)
        for g in range(2)
        for c in range(2)
        for a in range(seq_count // 2)
    ]
    outer = along([(0, 1), (1, 0), (2, 3), (3, 2)])
    inner = along([(1, 2), (2, 1)])
    outward_steps = along([(1, 0), (2, 3)])

    def send(value, pairs):
        return lax.ppermute(value, line_axes, pairs)

    swap_cores = [(i, i ^ 1) for i in range(seq_count)]
    swap_edges = [(i, i + 1) for i in range(1, seq_count - 1, 2)] + [
        (i + 1, i) for i in range(1, seq_count - 1, 2)
    ]

    by_kind = jnp.transpose(qkv_weight[0], (1, 0, 2))
    unit_heads = part // head // 6
    cuts = [0, 2, 4, 6]
    cuts = [cut * unit_heads * head for cut in cuts]

    def columns(index):
        begin, size = cuts[index], cuts[index + 1] - cuts[index]
        return lax.dynamic_slice(
            by_kind, (0, 0, mine * part + begin), (3, rows, size)
        )

    home = [columns(index) for index in range(3)]
    lent = lax.dynamic_slice(by_kind, (0, 0, (1 - mine) * part), (3, rows, part))

    def lend(pairs):
        pairs = [
            (a * section_count + section_count - 1, b * section_count) for a, b in pairs
        ]
        return lax.ppermute(stream, ("seq", "section"), pairs)

    pair = lax.ppermute(stream, "seq", swap_cores)
    halo = lend(swap_edges)
    pair_halo = lend([(a, b ^ 1) for a, b in swap_edges])
    home_pair = lax.ppermute(lent, "seq", swap_cores)

    crossings = []

    def cross(value):
        if len(crossings) >= 2:
            value = tied(value, crossings[-2])
        crossings.append(send(value, opposite))
        return crossings[-1]

    from_outer, from_inner = [], []
    across_first, inner_next, outer_next = [], [], []
    for kind in range(3):
        ready = home[kind]
        if kind == 1:
            ready = tied(ready, pair)
        if kind == 2:
            ready = tied(ready, from_outer[0], from_inner[0])
        from_outer.append(send(ready, outer))
        from_inner.append(send(ready, inner))
    before = ()
    for kind in range(3):
        a = tied(from_outer[kind], from_inner[kind], *before)
        b = tied(from_inner[kind], from_outer[kind], *before)
        across_first.append(cross(a))
        inner_next.append(send(a, inner))
        outer_next.append(send(b, outward_steps))
        before = (from_outer[kind], from_inner[kind])
    second, across_second, outer_last = [], [], []
    for kind in range(3):
        before = before + (across_first[kind],)
        a = tied(inner_next[kind], outer_next[kind], *before)
        b = tied(outer_next[kind], inner_next[kind], *before)
        outer_last.append(send(a, outward_steps))
        second.append(jnp.where(middle, from_inner[kind], b))
        across_second.append(cross(second[kind]))
        before = (inner_next[kind], outer_next[kind])
    third, across_third = [], []
    for kind in range(3):
        a = tied(outer_last[kind], across_second[kind], *before)
        third.append(jnp.where(middle, inner_next[kind], a))
        across_third.append(cross(third[kind]))
        before = (outer_last[kind],)

    section_place = lax.axis_index("section")
    gates = jnp.transpose(set_gate[0], (1, 0, 2))

    vmem = pl.BlockSpec(memory_space=pltpu.VMEM)
    smem = pl.BlockSpec(memory_space=pltpu.SMEM)
    anywhere = pl.BlockSpec(memory_space=pl.ANY)
    half_shape = jax.ShapeDtypeStruct((micro_count, view_tok, part), jnp.bfloat16)
    normed_shape = (4 * micro_count * view_tok, width)
    mega = 1024 * 1024

    def limit(size):
        return pltpu.CompilerParams(vmem_limit_bytes=size * mega)

    norm = pl.pallas_call(
        norm_kernel,
        out_shape=jax.ShapeDtypeStruct(normed_shape, jnp.bfloat16),
        in_specs=[smem] + [vmem] * 5,
        out_specs=vmem,
        compiler_params=limit(12),
        name="norm",
    )

    def attend_part(index, normed, pieces, earlier):
        return pl.pallas_call(
            functools.partial(attend_part_kernel, cuts[index]),
            out_shape=(
                half_shape,
                half_shape,
                jax.ShapeDtypeStruct(
                    (width, 3 * (cuts[index + 1] - cuts[index])), jnp.bfloat16
                ),
            ),
            in_specs=[smem, vmem, vmem] + [anywhere] * 8 + [vmem] * len(earlier),
            out_specs=(vmem, vmem, vmem),
            scratch_shapes=[pltpu.SemaphoreType.DMA((24,))],
            input_output_aliases={11: 0, 12: 1} if earlier else {},
            compiler_params=limit(20),
            name="attend_part",
        )(set_views, normed, norm_gain[0], *pieces, *earlier)

    attend = pl.pallas_call(
        attend_kernel,
        out_shape=(half_shape, half_shape),
        in_specs=[smem] + [anywhere] * 4 + [vmem] * 5,
        out_specs=(vmem, vmem),
        scratch_shapes=[
            pltpu.VMEM(normed_shape, jnp.bfloat16),
            pltpu.VMEM((4,) + stream.shape, jnp.bfloat16),
            pltpu.SemaphoreType.DMA((4,)),
        ],
        compiler_params=limit(24),
        name="attend",
    )

    def project(last, *operands):
        spare = [pltpu.VMEM(stream.shape, jnp.bfloat16)] if last else []
        in_specs = [smem] + [anywhere] * 4 + [vmem] + [anywhere] * last
        return pl.pallas_call(
            functools.partial(project_kernel, last),
            out_shape=jax.ShapeDtypeStruct(stream.shape, jnp.bfloat16),
            in_specs=in_specs,
            out_specs=vmem,
            scratch_shapes=[
                pltpu.VMEM((micro_count, view_tok, part), jnp.bfloat16),
                pltpu.VMEM((micro_count, view_tok, part), jnp.bfloat16),
                pltpu.VMEM(stream.shape, jnp.bfloat16),
                pltpu.VMEM(gates.shape, jnp.bfloat16),
            ]
            + spare
            + [pltpu.SemaphoreType.DMA((5,))],
            compiler_params=limit(12),
            name="project",
        )(*operands)

    own = stream
    hidden = None
    for moment in range(section_count):
        if moment > 0:
            halo = lax.ppermute(own, "seq", swap_edges)
            pair = lax.ppermute(own, "seq", swap_cores)
            pair_halo = lax.ppermute(halo, "seq", swap_cores)
            att_own, att_pair = attend(
                set_views,
                own,
                pair,
                halo,
                pair_halo,
                modulation[0],
                norm_gain[0],
                *assembled,
            )
        else:
            normed = norm(set_views, own, pair, halo, pair_halo, modulation[0])
            earlier, assembled = (), []
            for index in range(3):
                pieces = [
                    home[index],
                    home_pair,
                    from_outer[index],
                    across_first[index],
                    second[index],
                    across_second[index],
                    third[index],
                    across_third[index],
                ]
                *earlier, joined = attend_part(index, normed, pieces, earlier)
                assembled.append(joined)
            att_own, att_pair = earlier
        att_got = lax.ppermute(att_pair, "seq", swap_cores)
        operands = (set_views, att_own, att_got, own, gates, out_weight[0])
        if moment > 0 and moment + 1 == section_count:
            hidden = project(True, *operands, hidden)
        else:
            result = project(False, *operands)
            if moment == 0:
                hidden = result
            else:
                hidden = jnp.where(section_place == moment, result, hidden)
        if moment + 1 < section_count:
            own = lax.ppermute(
                result, "section", [(i, i + 1) for i in range(section_count - 1)]
            )
    return hidden[None]


def shifted(array, axis, by):
    size = lax.axis_size(axis)
    pairs = [(i, i + by) for i in range(size) if 0 <= i + by < size]
    return lax.ppermute(array, axis, pairs)


def unit_rms(values, scaling):
    return (
        values
        * lax.rsqrt(jnp.mean(values * values, axis=-1, keepdims=True) + epsilon)
        * scaling
    )


def general_body(
    stream, set_views, modulation, set_gate, qkv_weight, norm_gain, out_weight
):
    micro_count, view_tok, local_width = stream.shape
    head_size = norm_gain.shape[2]
    head_count = local_width // head_size
    seq_count = lax.axis_size("seq")
    section_count = lax.axis_size("section")
    seq_place = lax.axis_index("seq")
    section_place = lax.axis_index("section")
    full_width = local_width * lax.axis_size("tp")
    whole_qkv = lax.all_gather(qkv_weight[0], "seq", axis=0, tiled=True)
    qkv_flat = whole_qkv.reshape(whole_qkv.shape[0], 3 * local_width)
    gain_pair = norm_gain[0]
    out_rows = out_weight[0]
    score_scale = head_size ** (-0.5)
    offsets = list(range(-REACH, REACH + 1))
    ticks = micro_count + section_count - 1
    carried = jnp.zeros((view_tok, local_width), jnp.bfloat16)
    hidden = jnp.zeros((micro_count, view_tok, local_width), jnp.bfloat16)
    for moment in range(ticks):
        fresh_input = stream[min(moment, micro_count - 1)]
        section_input = jnp.where(section_place == 0, fresh_input, carried)
        micro_raw = moment - section_place
        micro_index = jnp.clip(micro_raw, 0, micro_count - 1)
        owners = view_sets(set_views[micro_index], seq_count)
        own_set = owners[seq_place]
        widened = section_input.astype(jnp.float32)
        totals, squares = lax.psum(
            (jnp.sum(widened, axis=1), jnp.sum(widened * widened, axis=1)), "tp"
        )
        average = (totals / full_width)[:, None]
        spread = (squares / full_width)[:, None] - average * average
        factors = modulation[0, micro_index, own_set].astype(jnp.float32)
        normed = (
            (widened - average) * lax.rsqrt(spread + epsilon) * (1.0 + factors[1])
            + factors[0]
        ).astype(jnp.bfloat16)
        projected = jnp.dot(
            lax.all_gather(normed, "tp", axis=1, tiled=True),
            qkv_flat,
            preferred_element_type=jnp.float32,
        )
        parts = projected.reshape(view_tok, 3, head_count, head_size)
        queries = unit_rms(parts[:, 0], gain_pair[0]).astype(jnp.bfloat16)
        keys_here = unit_rms(parts[:, 1], gain_pair[1]).astype(jnp.bfloat16)
        values_here = parts[:, 2].astype(jnp.bfloat16)
        payload = jnp.stack(
            [
                keys_here.reshape(view_tok, local_width),
                values_here.reshape(view_tok, local_width),
            ]
        )
        arrived = [shifted(payload, "seq", 1), payload, shifted(payload, "seq", -1)]
        key_list = [r[0].reshape(view_tok, head_count, head_size) for r in arrived]
        value_list = [r[1].reshape(view_tok, head_count, head_size) for r in arrived]
        visible = []
        for offset in offsets:
            neighbour = seq_place + offset
            in_range = (neighbour >= 0) & (neighbour < seq_count)
            same_set = owners[jnp.clip(neighbour, 0, seq_count - 1)] == own_set
            visible.append((in_range & same_set).astype(jnp.float32))
        keys_cat = jnp.concatenate(key_list, axis=0)
        values_cat = jnp.concatenate(value_list, axis=0)
        mask_row = jnp.repeat(jnp.stack(visible), view_tok)
        scores = (
            jnp.einsum(
                "qhd,khd->hqk", queries, keys_cat, preferred_element_type=jnp.float32
            )
            * score_scale
        )
        exponent = jnp.exp(scores) * mask_row
        denominator = jnp.sum(exponent, axis=-1)
        numerator = jnp.einsum(
            "hqk,khd->qhd",
            exponent.astype(jnp.bfloat16),
            values_cat,
            preferred_element_type=jnp.float32,
        )
        attended = (
            (numerator / jnp.transpose(denominator)[:, :, None])
            .astype(jnp.bfloat16)
            .reshape(view_tok, local_width)
        )
        mixed_out = jnp.dot(
            lax.all_gather(attended, "tp", axis=1, tiled=True),
            out_rows,
            preferred_element_type=jnp.float32,
        )
        gating = set_gate[0, micro_index, own_set].astype(jnp.float32)
        result = (widened + gating * mixed_out).astype(jnp.bfloat16)
        in_range = (micro_raw >= 0) & (micro_raw < micro_count)
        hidden = jnp.where(in_range, hidden.at[micro_index].set(result), hidden)
        if moment + 1 < ticks:
            carried = shifted(result, "section", 1)
    return hidden[None]


def solution(mesh):
    placed = (
        P("groups", "seq", "tp"),
        P("groups", None),
        P("section", "groups", None, None, "tp"),
        P("section", "groups", None, "tp"),
        P("section", "seq", None, "tp"),
        P("section", None, None),
        P("section", None, "tp"),
    )
    sizes = mesh.shape
    paired = sizes["tp"] == 1 and sizes["groups"] == 2 and sizes["seq"] == 8
    return jax.shard_map(
        paired_body if paired else general_body,
        mesh=mesh,
        in_specs=placed,
        out_specs=P("section", "groups", "seq", "tp"),
        check_vma=False,
    )
```

```python
import functools

import jax
import jax.numpy as jnp
from jax import lax
from jax.experimental import pallas as pl
from jax.experimental.pallas import tpu as pltpu
from jax.sharding import PartitionSpec as P

REACH = 1


epsilon = 1e-06


def view_sets(set_views, count):
    amount = set_views.shape[0]
    before = jnp.arange(amount)[:, None] > jnp.arange(amount)[None, :]
    starts = jnp.sum(jnp.where(before, set_views[None, :], 0), axis=1)
    position = jnp.arange(count, dtype=jnp.int32)
    inside = (starts[None, :] <= position[:, None]).astype(jnp.int32)
    return jnp.sum(inside, axis=1) - 1


def owner_of(views, m, place):
    start, owner = jnp.int32(0), jnp.int32(-1)
    for j in range(views.shape[1]):
        owner = owner + jnp.where(start <= place, 1, 0)
        start = start + views[m, j]
    return owner


def attend_table(views):
    count = lax.axis_size("seq")
    place = lax.axis_index("seq")
    core = place % 2
    chip = place // 2
    middle = (chip == 1) | (chip == 2)
    others = (
        chip,
        chip + 1 - 2 * (chip % 2),
        jnp.where(middle, 3 - chip, (chip + 2) % 4),
        jnp.where(middle, jnp.where(chip == 1, 3, 0), 3 - chip),
    )
    order = []
    for other in others:
        order += [2 * other + core, 2 * other + 1 - core]
    outward = 2 * core - 1
    pair_place = place - outward
    halo_place = place + outward
    pair_halo_place = pair_place - outward
    places = (place, pair_place, halo_place, pair_halo_place)
    sets, masks = [], []
    for m in range(views.shape[0]):
        found = [
            owner_of(views, m, jnp.clip(where, 0, count - 1)) for where in places
        ]
        sets.append(found)
        masks.append(
            (
                found[0] == found[1],
                (halo_place >= 0) & (halo_place < count) & (found[0] == found[2]),
                (pair_halo_place >= 0)
                & (pair_halo_place < count)
                & (found[1] == found[3]),
            )
        )
    return order, sets, masks


def normalise(source, m, slot, modulation, sets, normed, dtype=jnp.bfloat16):
    micro_count, view_tok, _ = source.shape
    wide = source[m].astype(jnp.float32)
    average = jnp.mean(wide, axis=-1, keepdims=True)
    squares = jnp.mean(wide * wide, axis=-1, keepdims=True)
    spread = squares - average * average
    factors = modulation[m, sets[m][slot]].astype(jnp.float32)
    value = (wide - average) * lax.rsqrt(spread + epsilon) * (
        1.0 + factors[1:2]
    ) + factors[0:1]
    half = 2 * micro_count * view_tok
    first = half * (slot // 2) + (2 * m + slot % 2) * view_tok
    normed[first : first + view_tok, :] = value.astype(dtype)


def norm_kernel(views, own, pair, halo, pair_halo, modulation, normed):
    _, sets, _ = attend_table(views)
    for slot, source in enumerate((own, pair, halo, pair_halo)):
        for m in range(source.shape[0]):
            normalise(source, m, slot, modulation, sets, normed)


def set_masks(masks, view_tok):
    two = 2 * view_tok
    low_row = lax.broadcasted_iota(jnp.int32, (two, two), 0) < view_tok
    low_col = lax.broadcasted_iota(jnp.int32, (two, two), 1) < view_tok
    near_masks, far_masks = [], []
    for found in masks:
        together, below, above = (jnp.where(mask, 1.0, 0.0) for mask in found)
        near_masks.append(jnp.where(low_row == low_col, 1.0, together))
        far_masks.append(
            jnp.where(
                low_row & low_col,
                below,
                jnp.where(low_row | low_col, 0.0, above),
            )
        )
    return near_masks, far_masks


def unit_rows(values, gain):
    scale = lax.rsqrt(jnp.mean(values * values, axis=-1, keepdims=True) + epsilon)
    return (values * scale * gain).astype(jnp.bfloat16)


def dot(a, b):
    return jnp.dot(a, b, preferred_element_type=jnp.float32)


def exponents(queries, keys, mask):
    scores = lax.dot_general(
        queries, keys, (((1,), (1,)), ((), ())), preferred_element_type=jnp.float32
    )
    return jnp.exp(scores * queries.shape[1] ** (-0.5)) * mask


def raw_heads(normed, weights, micro_count, view_tok):
    part = weights.shape[1] // 3
    half = 2 * micro_count * view_tok
    return (
        dot(normed[0:half, :], weights[:, 0:part]),
        dot(normed[...], weights[:, part : 2 * part]),
        dot(normed[...], weights[:, 2 * part : 3 * part]),
    )


def attend_heads(raw, gains, near_masks, far_masks, view_tok, outputs):
    raw_q, raw_k, raw_v = raw
    micro_count = len(near_masks)
    part = raw_q.shape[1]
    head = gains.shape[1]
    two = 2 * view_tok
    half = micro_count * two
    att_own, att_pair, offset = outputs
    cases = []
    for i in range(part // head):
        cols = slice(i * head, (i + 1) * head)
        queries = unit_rows(raw_q[:, cols], gains[0:1, :])
        keys = unit_rows(raw_k[:, cols], gains[1:2, :])
        values = raw_v[:, cols].astype(jnp.bfloat16)
        for m in range(micro_count):
            near = slice(m * two, (m + 1) * two)
            far = slice(half + m * two, half + (m + 1) * two)
            cases.append((i, m, queries[near], keys, values, near, far))
    weights = []
    for i, m, queries, keys, values, near, far in cases:
        weights.append(
            (
                exponents(queries, keys[near], near_masks[m]),
                exponents(queries, keys[far], far_masks[m]),
            )
        )
    for case, (e_near, e_far) in zip(cases, weights):
        i, m, queries, keys, values, near, far = case
        total = jnp.sum(e_near, axis=-1, keepdims=True) + jnp.sum(
            e_far, axis=-1, keepdims=True
        )
        mixed = dot(e_near.astype(jnp.bfloat16), values[near]) + dot(
            e_far.astype(jnp.bfloat16), values[far]
        )
        attended = (mixed / total).astype(jnp.bfloat16)
        put = slice(offset + i * head, offset + (i + 1) * head)
        att_own[m, :, put] = attended[:view_tok]
        att_pair[m, :, put] = attended[view_tok:]


def attend_part_kernel(offset, *refs):
    views, normed, gains = refs[:3]
    pieces = refs[3:11]
    att_own, att_pair, weights, sems = refs[-4:]
    rows, part = pieces[0].shape[1:]
    view_tok = att_own.shape[1]
    order, _, masks = attend_table(views)
    moves = []
    for slot in range(8):
        start = pl.multiple_of(order[slot] * rows, rows)
        for kind in range(3):
            source = pieces[slot].at[kind]
            if slot == 1:
                source = source.at[:, pl.ds(offset, part)]
            moves.append(
                pltpu.make_async_copy(
                    source,
                    weights.at[pl.ds(start, rows), pl.ds(kind * part, part)],
                    sems.at[3 * slot + kind],
                )
            )
    for move in moves:
        move.start()
    near_masks, far_masks = set_masks(masks, view_tok)
    for move in moves:
        move.wait()
    attend_heads(
        raw_heads(normed, weights, att_own.shape[0], view_tok),
        gains,
        near_masks,
        far_masks,
        view_tok,
        (att_own, att_pair, offset),
    )


def attend_kernel(*refs):
    views, own, pair, halo, pair_halo, modulation, gains = refs[:7]
    weights = refs[7:10]
    att_own, att_pair, normed, streams, sems = refs[10:]
    micro_count, view_tok, _ = own.shape
    _, sets, masks = attend_table(views)
    incoming = [
        pltpu.make_async_copy(source, streams.at[slot], sems.at[slot])
        for slot, source in enumerate((own, pair, halo, pair_halo))
    ]
    for move in incoming:
        move.start()
    near_masks, far_masks = set_masks(masks, view_tok)
    for slot in range(4):
        incoming[slot].wait()
        for m in range(micro_count):
            normalise(streams.at[slot], m, slot, modulation, sets, normed)
    offset = 0
    raw = raw_heads(normed, weights[0], micro_count, view_tok)
    for index in range(3):
        current = raw
        if index < 2:
            raw = raw_heads(normed, weights[index + 1], micro_count, view_tok)
        attend_heads(
            current,
            gains,
            near_masks,
            far_masks,
            view_tok,
            (att_own, att_pair, offset),
        )
        offset += weights[index].shape[1] // 3


def project_kernel(last, *refs):
    views, att_own_src, att_got_src, stream_src, gates_src, out_weight = refs[:6]
    refs = refs[6:]
    if last:
        keep_src, refs = refs[0], refs[1:]
    result, att_own, att_got, stream, gates = refs[:5]
    refs = refs[5:]
    if last:
        keep, refs = refs[0], refs[1:]
    (small_sems,) = refs
    micro_count, view_tok, part = att_own.shape
    width = out_weight.shape[1]
    place = lax.axis_index("seq")
    mine = (place + lax.axis_index("groups")) % 2
    newest = lax.axis_index("section") == lax.axis_size("section") - 1
    sets = [owner_of(views, m, place) for m in range(views.shape[0])]
    blocks = 3
    block = width // blocks

    moves = [
        (att_own_src, att_own),
        (att_got_src, att_got),
        (stream_src, stream),
        (gates_src, gates),
    ]
    if last:
        moves.append((keep_src, keep))
    copies = [
        pltpu.make_async_copy(source, target, small_sems.at[i])
        for i, (source, target) in enumerate(moves)
    ]
    for copy in copies:
        copy.start()
    for copy in copies[:2]:
        copy.wait()
    tokens = micro_count * view_tok
    here = att_own[...].reshape(tokens, part)
    there = att_got[...].reshape(tokens, part)
    first = pl.multiple_of(mine * part, part)
    second = pl.multiple_of((1 - mine) * part, part)
    for index in range(blocks):
        cols = slice(index * block, (index + 1) * block)
        mixed = jnp.dot(
            here, out_weight[pl.ds(first, part), cols], preferred_element_type=jnp.float32
        ) + jnp.dot(
            there,
            out_weight[pl.ds(second, part), cols],
            preferred_element_type=jnp.float32,
        )
        if index == 0:
            for copy in copies[2:]:
                copy.wait()
        for m in range(micro_count):
            gate = gates[sets[m]][m : m + 1, cols].astype(jnp.float32)
            value = (
                stream[m, :, cols].astype(jnp.float32)
                + gate * mixed[m * view_tok : (m + 1) * view_tok]
            ).astype(jnp.bfloat16)
            if last:
                value = jnp.where(newest, value, keep[m, :, cols])
            result[m, :, cols] = value


def tied(value, *others):
    return lax.optimization_barrier((value,) + others)[0]


def paired_body(
    stream, set_views, modulation, set_gate, qkv_weight, norm_gain, out_weight
):
    micro_count, view_tok, width = stream.shape
    head = norm_gain.shape[2]
    part = width // 2
    rows = qkv_weight.shape[1]
    seq_count = lax.axis_size("seq")
    section_count = lax.axis_size("section")
    group = lax.axis_index("groups")
    place = lax.axis_index("seq")
    core = place % 2
    chip = place // 2
    mine = core ^ group
    middle = (chip == 1) | (chip == 2)
    line_axes = ("groups", "seq")

    def along(steps):
        return [
            (g * seq_count + 2 * a + c, g * seq_count + 2 * b + c)
            for g in range(2)
            for c in range(2)
            for a, b in steps
        ]

    opposite = [
        (g * seq_count + 2 * a + c, (1 - g) * seq_count + 2 * a + 1 - c)
        for g in range(2)
        for c in range(2)
        for a in range(seq_count // 2)
    ]
    outer = along([(0, 1), (1, 0), (2, 3), (3, 2)])
    inner = along([(1, 2), (2, 1)])
    outward_steps = along([(1, 0), (2, 3)])

    def send(value, pairs):
        return lax.ppermute(value, line_axes, pairs)

    swap_cores = [(i, i ^ 1) for i in range(seq_count)]
    swap_edges = [(i, i + 1) for i in range(1, seq_count - 1, 2)] + [
        (i + 1, i) for i in range(1, seq_count - 1, 2)
    ]

    by_kind = jnp.transpose(qkv_weight[0], (1, 0, 2))
    unit_heads = part // head // 6
    cuts = [0, 2, 4, 6]
    cuts = [cut * unit_heads * head for cut in cuts]

    def columns(index):
        begin, size = cuts[index], cuts[index + 1] - cuts[index]
        return lax.dynamic_slice(
            by_kind, (0, 0, mine * part + begin), (3, rows, size)
        )

    home = [columns(index) for index in range(3)]
    lent = lax.dynamic_slice(by_kind, (0, 0, (1 - mine) * part), (3, rows, part))

    def lend(pairs):
        pairs = [
            (a * section_count + section_count - 1, b * section_count) for a, b in pairs
        ]
        return lax.ppermute(stream, ("seq", "section"), pairs)

    pair = lax.ppermute(stream, "seq", swap_cores)
    halo = lend(swap_edges)
    pair_halo = lend([(a, b ^ 1) for a, b in swap_edges])
    home_pair = lax.ppermute(lent, "seq", swap_cores)

    crossings = []

    def cross(value):
        if len(crossings) >= 2:
            value = tied(value, crossings[-2])
        crossings.append(send(value, opposite))
        return crossings[-1]

    from_outer, from_inner = [], []
    across_first, inner_next, outer_next = [], [], []
    for kind in range(3):
        ready = home[kind]
        if kind == 1:
            ready = tied(ready, pair)
        if kind == 2:
            ready = tied(ready, from_outer[0], from_inner[0])
        from_outer.append(send(ready, outer))
        from_inner.append(send(ready, inner))
    before = ()
    for kind in range(3):
        a = tied(from_outer[kind], from_inner[kind], *before)
        b = tied(from_inner[kind], from_outer[kind], *before)
        across_first.append(cross(a))
        inner_next.append(send(a, inner))
        outer_next.append(send(b, outward_steps))
        before = (from_outer[kind], from_inner[kind])
    second, across_second, outer_last = [], [], []
    for kind in range(3):
        before = before + (across_first[kind],)
        a = tied(inner_next[kind], *before)
        b = tied(outer_next[kind], *before)
        outer_last.append(send(a, outward_steps))
        second.append(jnp.where(middle, from_inner[kind], b))
        across_second.append(cross(second[kind]))
        before = (inner_next[kind], outer_next[kind])
    third, across_third = [], []
    for kind in range(3):
        a = tied(outer_last[kind], across_second[kind], *before)
        third.append(jnp.where(middle, inner_next[kind], a))
        across_third.append(cross(third[kind]))
        before = (outer_last[kind],)

    section_place = lax.axis_index("section")
    gates = jnp.transpose(set_gate[0], (1, 0, 2))

    vmem = pl.BlockSpec(memory_space=pltpu.VMEM)
    smem = pl.BlockSpec(memory_space=pltpu.SMEM)
    anywhere = pl.BlockSpec(memory_space=pl.ANY)
    half_shape = jax.ShapeDtypeStruct((micro_count, view_tok, part), jnp.bfloat16)
    normed_shape = (4 * micro_count * view_tok, width)
    mega = 1024 * 1024

    def limit(size):
        return pltpu.CompilerParams(vmem_limit_bytes=size * mega)

    norm = pl.pallas_call(
        norm_kernel,
        out_shape=jax.ShapeDtypeStruct(normed_shape, jnp.bfloat16),
        in_specs=[smem] + [vmem] * 5,
        out_specs=vmem,
        compiler_params=limit(12),
        name="norm",
    )

    def attend_part(index, normed, pieces, earlier):
        return pl.pallas_call(
            functools.partial(attend_part_kernel, cuts[index]),
            out_shape=(
                half_shape,
                half_shape,
                jax.ShapeDtypeStruct(
                    (width, 3 * (cuts[index + 1] - cuts[index])), jnp.bfloat16
                ),
            ),
            in_specs=[smem, vmem, vmem] + [anywhere] * 8 + [vmem] * len(earlier),
            out_specs=(vmem, vmem, vmem),
            scratch_shapes=[pltpu.SemaphoreType.DMA((24,))],
            input_output_aliases={11: 0, 12: 1} if earlier else {},
            compiler_params=limit(20),
            name="attend_part",
        )(set_views, normed, norm_gain[0], *pieces, *earlier)

    attend = pl.pallas_call(
        attend_kernel,
        out_shape=(half_shape, half_shape),
        in_specs=[smem] + [anywhere] * 4 + [vmem] * 5,
        out_specs=(vmem, vmem),
        scratch_shapes=[
            pltpu.VMEM(normed_shape, jnp.bfloat16),
            pltpu.VMEM((4,) + stream.shape, jnp.bfloat16),
            pltpu.SemaphoreType.DMA((4,)),
        ],
        compiler_params=limit(24),
        name="attend",
    )

    def project(last, *operands):
        spare = [pltpu.VMEM(stream.shape, jnp.bfloat16)] if last else []
        in_specs = [smem] + [anywhere] * 4 + [vmem] + [anywhere] * last
        return pl.pallas_call(
            functools.partial(project_kernel, last),
            out_shape=jax.ShapeDtypeStruct(stream.shape, jnp.bfloat16),
            in_specs=in_specs,
            out_specs=vmem,
            scratch_shapes=[
                pltpu.VMEM((micro_count, view_tok, part), jnp.bfloat16),
                pltpu.VMEM((micro_count, view_tok, part), jnp.bfloat16),
                pltpu.VMEM(stream.shape, jnp.bfloat16),
                pltpu.VMEM(gates.shape, jnp.bfloat16),
            ]
            + spare
            + [pltpu.SemaphoreType.DMA((5,))],
            compiler_params=limit(12),
            name="project",
        )(*operands)

    own = stream
    hidden = None
    for moment in range(section_count):
        if moment > 0:
            halo = lax.ppermute(own, "seq", swap_edges)
            pair = lax.ppermute(own, "seq", swap_cores)
            pair_halo = lax.ppermute(halo, "seq", swap_cores)
            att_own, att_pair = attend(
                set_views,
                own,
                pair,
                halo,
                pair_halo,
                modulation[0],
                norm_gain[0],
                *assembled,
            )
        else:
            normed = norm(set_views, own, pair, halo, pair_halo, modulation[0])
            earlier, assembled = (), []
            for index in range(3):
                pieces = [
                    home[index],
                    home_pair,
                    from_outer[index],
                    across_first[index],
                    second[index],
                    across_second[index],
                    third[index],
                    across_third[index],
                ]
                *earlier, joined = attend_part(index, normed, pieces, earlier)
                assembled.append(joined)
            att_own, att_pair = earlier
        att_got = lax.ppermute(att_pair, "seq", swap_cores)
        operands = (set_views, att_own, att_got, own, gates, out_weight[0])
        if moment > 0 and moment + 1 == section_count:
            hidden = project(True, *operands, hidden)
        else:
            result = project(False, *operands)
            if moment == 0:
                hidden = result
            else:
                hidden = jnp.where(section_place == moment, result, hidden)
        if moment + 1 < section_count:
            own = lax.ppermute(
                result, "section", [(i, i + 1) for i in range(section_count - 1)]
            )
    return hidden[None]


def shifted(array, axis, by):
    size = lax.axis_size(axis)
    pairs = [(i, i + by) for i in range(size) if 0 <= i + by < size]
    return lax.ppermute(array, axis, pairs)


def unit_rms(values, scaling):
    return (
        values
        * lax.rsqrt(jnp.mean(values * values, axis=-1, keepdims=True) + epsilon)
        * scaling
    )


def general_body(
    stream, set_views, modulation, set_gate, qkv_weight, norm_gain, out_weight
):
    micro_count, view_tok, local_width = stream.shape
    head_size = norm_gain.shape[2]
    head_count = local_width // head_size
    seq_count = lax.axis_size("seq")
    section_count = lax.axis_size("section")
    seq_place = lax.axis_index("seq")
    section_place = lax.axis_index("section")
    full_width = local_width * lax.axis_size("tp")
    whole_qkv = lax.all_gather(qkv_weight[0], "seq", axis=0, tiled=True)
    qkv_flat = whole_qkv.reshape(whole_qkv.shape[0], 3 * local_width)
    gain_pair = norm_gain[0]
    out_rows = out_weight[0]
    score_scale = head_size ** (-0.5)
    offsets = list(range(-REACH, REACH + 1))
    ticks = micro_count + section_count - 1
    carried = jnp.zeros((view_tok, local_width), jnp.bfloat16)
    hidden = jnp.zeros((micro_count, view_tok, local_width), jnp.bfloat16)
    for moment in range(ticks):
        fresh_input = stream[min(moment, micro_count - 1)]
        section_input = jnp.where(section_place == 0, fresh_input, carried)
        micro_raw = moment - section_place
        micro_index = jnp.clip(micro_raw, 0, micro_count - 1)
        owners = view_sets(set_views[micro_index], seq_count)
        own_set = owners[seq_place]
        widened = section_input.astype(jnp.float32)
        totals, squares = lax.psum(
            (jnp.sum(widened, axis=1), jnp.sum(widened * widened, axis=1)), "tp"
        )
        average = (totals / full_width)[:, None]
        spread = (squares / full_width)[:, None] - average * average
        factors = modulation[0, micro_index, own_set].astype(jnp.float32)
        normed = (
            (widened - average) * lax.rsqrt(spread + epsilon) * (1.0 + factors[1])
            + factors[0]
        ).astype(jnp.bfloat16)
        projected = jnp.dot(
            lax.all_gather(normed, "tp", axis=1, tiled=True),
            qkv_flat,
            preferred_element_type=jnp.float32,
        )
        parts = projected.reshape(view_tok, 3, head_count, head_size)
        queries = unit_rms(parts[:, 0], gain_pair[0]).astype(jnp.bfloat16)
        keys_here = unit_rms(parts[:, 1], gain_pair[1]).astype(jnp.bfloat16)
        values_here = parts[:, 2].astype(jnp.bfloat16)
        payload = jnp.stack(
            [
                keys_here.reshape(view_tok, local_width),
                values_here.reshape(view_tok, local_width),
            ]
        )
        arrived = [shifted(payload, "seq", 1), payload, shifted(payload, "seq", -1)]
        key_list = [r[0].reshape(view_tok, head_count, head_size) for r in arrived]
        value_list = [r[1].reshape(view_tok, head_count, head_size) for r in arrived]
        visible = []
        for offset in offsets:
            neighbour = seq_place + offset
            in_range = (neighbour >= 0) & (neighbour < seq_count)
            same_set = owners[jnp.clip(neighbour, 0, seq_count - 1)] == own_set
            visible.append((in_range & same_set).astype(jnp.float32))
        keys_cat = jnp.concatenate(key_list, axis=0)
        values_cat = jnp.concatenate(value_list, axis=0)
        mask_row = jnp.repeat(jnp.stack(visible), view_tok)
        scores = (
            jnp.einsum(
                "qhd,khd->hqk", queries, keys_cat, preferred_element_type=jnp.float32
            )
            * score_scale
        )
        exponent = jnp.exp(scores) * mask_row
        denominator = jnp.sum(exponent, axis=-1)
        numerator = jnp.einsum(
            "hqk,khd->qhd",
            exponent.astype(jnp.bfloat16),
            values_cat,
            preferred_element_type=jnp.float32,
        )
        attended = (
            (numerator / jnp.transpose(denominator)[:, :, None])
            .astype(jnp.bfloat16)
            .reshape(view_tok, local_width)
        )
        mixed_out = jnp.dot(
            lax.all_gather(attended, "tp", axis=1, tiled=True),
            out_rows,
            preferred_element_type=jnp.float32,
        )
        gating = set_gate[0, micro_index, own_set].astype(jnp.float32)
        result = (widened + gating * mixed_out).astype(jnp.bfloat16)
        in_range = (micro_raw >= 0) & (micro_raw < micro_count)
        hidden = jnp.where(in_range, hidden.at[micro_index].set(result), hidden)
        if moment + 1 < ticks:
            carried = shifted(result, "section", 1)
    return hidden[None]


def solution(mesh):
    placed = (
        P("groups", "seq", "tp"),
        P("groups", None),
        P("section", "groups", None, None, "tp"),
        P("section", "groups", None, "tp"),
        P("section", "seq", None, "tp"),
        P("section", None, None),
        P("section", None, "tp"),
    )
    sizes = mesh.shape
    paired = sizes["tp"] == 1 and sizes["groups"] == 2 and sizes["seq"] == 8
    return jax.shard_map(
        paired_body if paired else general_body,
        mesh=mesh,
        in_specs=placed,
        out_specs=P("section", "groups", "seq", "tp"),
        check_vma=False,
    )
```
